32 devices in a mesh: band: 4 (over x, core), grid: 8 (over z, y).
Axes of the slice: x: 2, y: 2, z: 4, core: 2. Of those that a mesh axis runs over, the one named last changes fastest.
Arguments:
- orbitals: float32 [4, 128, 128, 128], P('band', 'grid'), may hold values from -4 to 10, as said below
- pivots: int32 [4], replicated, may hold values from 0 to 2097151, as said below
- pattern: int32 [4, 4], replicated, may hold values from 0 to 1, as said below
Outputs:
- localized: float32 [4, 128, 128, 128], P('band', 'grid')
- exchange_term: float32 [4, 128, 128, 128], P('band', 'grid')
The draws below stay inside these ranges and needn't reach their ends.
Inputs may be any that keep to these rules, and one draw needn't show every extreme that they name: Values of the orbitals on the grid; the matrix of their values at the pivots has a Cholesky factorization. `pivots`: distinct flat cell indices; the first and the last cell of the grid are always among them. `pattern`: every diagonal entry is 1; each row holds 1 to 4 ones, some row exactly 4; the matrix holds exactly 8 ones.
All inputs are finite; a program needn't handle non-finite values.
Results may differ from the reference program's by a relative error of at most 0.0003.
Values sent between devices are 32-bit elements; how exact they have to be, the bound alone decides.
A program may use at most 64 MiB of HBM per device.

```python
import jax
import jax.numpy as jnp
from jax import lax

BAND_DEV = 1
NG = 128
MOST_PARTNERS = 4
MEAN_PARTNERS = 2
BLOCKS = 4
BANDS = 4


def pivot_cells(key):
    inner_key = jax.random.fold_in(key, 7)
    choose_key, order_key = jax.random.split(inner_key)
    total = NG * NG * NG
    middle = jax.random.choice(choose_key, total - 2, (BANDS - 2,), replace=False).astype(jnp.int32) + 1
    ends = jnp.array([0, total - 1], dtype=jnp.int32)
    joined = jnp.concatenate([ends, middle])
    return jax.random.permutation(order_key, joined).astype(jnp.int32)


def draw_pivots(key, part):
    return pivot_cells(key)


def draw_orbitals(key, part):
    pivot_list = pivot_cells(key)
    key_bulk, key_diag, key_spread = jax.random.split(jax.random.fold_in(key, 11), 3)
    values_bulk = jnp.clip(jax.random.normal(key_bulk, (BANDS, NG * NG * NG), jnp.float32), -4.0, 4.0)
    root_bands = float(BANDS) ** 0.5
    diagonal = jax.random.uniform(key_diag, (BANDS,), jnp.float32, 6.0, 10.0)
    spread = jax.random.uniform(key_spread, (BANDS, BANDS), jnp.float32, -1.0, 1.0) / root_bands
    on_diagonal = jnp.arange(BANDS)[:, None] == jnp.arange(BANDS)[None, :]
    matrix = jnp.where(on_diagonal, diagonal[None, :], spread)
    return values_bulk.at[:, pivot_list].set(matrix).reshape(BANDS, NG, NG, NG)


def draw_pattern(key, part):
    key_heavy, key_order, key_rows = jax.random.split(jax.random.fold_in(key, 23), 3)
    heavy_row = jax.random.randint(key_heavy, (), 0, BLOCKS)
    ordering = jax.random.permutation(key_order, BLOCKS - 1)
    surplus = MEAN_PARTNERS * BLOCKS - BLOCKS - MOST_PARTNERS + 1
    row_ids = jnp.arange(BLOCKS, dtype=jnp.int32)
    position = jnp.clip(jnp.where(row_ids < heavy_row, row_ids, row_ids - 1), 0, BLOCKS - 2)
    counts = jnp.where(row_ids == heavy_row, MOST_PARTNERS, 1 + (ordering[position] < surplus).astype(jnp.int32))

    def one_row(row_id, wanted):
        ranking = jax.random.permutation(jax.random.fold_in(key_rows, row_id), BLOCKS)
        ranking = jnp.where(row_ids == row_id, -1, ranking)
        places = jnp.sum(ranking[None, :] < ranking[:, None], axis=1)
        return (places < wanted).astype(jnp.int32)
    return jax.vmap(one_row)(row_ids, counts)


def setup_inputs(seed: int = 0) -> dict:
    seeds = jax.random.split(jax.random.key(seed), 4)
    orbitals = draw_orbitals(jax.random.fold_in(seeds[3], 71), 0)
    pivots = draw_pivots(jax.random.fold_in(seeds[3], 71), 0)
    pattern = draw_pattern(jax.random.fold_in(seeds[3], 71), 0)
    return dict(orbitals=orbitals, pivots=pivots, pattern=pattern)


precise = lax.Precision.HIGHEST

def wrapped(indices, length):
    return jnp.where(indices < length // 2, indices, indices - length)

def coulomb_kernel(length):
    waves = wrapped(jnp.arange(length, dtype=jnp.int32), length).astype(jnp.float32)
    squared = waves[:, None, None] ** 2 + waves[None, :, None] ** 2 + waves[None, None, :] ** 2
    scaling = float(length) ** 1.5
    return jnp.where(squared > 0, 0.25 / (scaling * jnp.maximum(squared, 1.0)), 0.0)

def reference(orbitals, pivots, pattern):
    flat_orbitals = orbitals.reshape(BANDS, NG * NG * NG)
    picked = jnp.take(flat_orbitals, pivots, axis=1)
    gram_matrix = jnp.dot(picked.T, picked, precision=precise)
    factor = jnp.linalg.cholesky(gram_matrix)
    rotation = lax.linalg.triangular_solve(factor, picked.T, left_side=True, lower=True).T
    localized = jnp.dot(rotation.T, flat_orbitals, precision=precise).reshape(BANDS, NG, NG, NG)
    kernel = coulomb_kernel(NG)
    volume = float(NG) ** 3
    band_block = jnp.arange(BANDS, dtype=jnp.int32) // BAND_DEV
    weights = pattern[band_block[:, None], band_block[None, :]].astype(localized.dtype)

    def one_band(inputs):
        single, weight_row = inputs
        density = single[None] * localized
        spectra = jnp.fft.fftn(density, axes=(1, 2, 3)) * kernel
        potential = jnp.real(jnp.fft.ifftn(spectra, axes=(1, 2, 3))) * volume
        return jnp.sum(weight_row[:, None, None, None] * potential * localized, axis=0)
    exchange_term = lax.map(one_band, (localized, weights))
    return (localized, exchange_term)
```

```python
import functools

import jax
import jax.numpy as jnp
import numpy as np
from jax import lax
from jax.experimental import pallas as pl
from jax.experimental.pallas import tpu as pltpu
from jax.sharding import PartitionSpec as P

precise = lax.Precision.HIGHEST
MESH = pl.DeviceIdType.MESH


def complex_table(length):
    across = np.arange(length)
    angles = (across[:, None] * across[None, :] % length) * (2.0 * np.pi / length)
    cosine, sine = np.cos(angles), np.sin(angles)
    return np.block([[cosine, -sine], [sine, cosine]]).astype(np.float32)


def wrapped(indices, length):
    return jnp.where(indices < length // 2, indices, indices - length)


def coulomb(length, row_start, row_count):
    wave = wrapped(jnp.arange(length, dtype=jnp.int32), length).astype(jnp.float32)
    rows = wrapped(row_start + jnp.arange(row_count, dtype=jnp.int32), length).astype(jnp.float32)
    squared = rows[:, None, None] ** 2 + wave[None, :, None] ** 2 + wave[None, None, :] ** 2
    scaling = float(length) ** 1.5
    return jnp.where(squared > 0, 0.25 / (scaling * jnp.maximum(squared, 1.0)), 0.0)


def times(left, right):
    return jnp.dot(left, right, precision=precise, preferred_element_type=jnp.float32)


def sum_kernel(n, bands, own_ref, out_ref, wide, from_grid, from_band, sems):
    grid_me, band_me = lax.axis_index("grid"), lax.axis_index("band")
    barrier = pltpu.get_barrier_semaphore()
    axes = (("grid", n, grid_me), ("band", bands, band_me))
    for axis, count, me in axes:
        for step in range(1, count):
            pl.semaphore_signal(
                barrier, inc=1, device_id={axis: lax.rem(me + step, count)}, device_id_type=MESH
            )
    pl.semaphore_wait(barrier, n + bands - 2)
    total = own_ref[...]
    for place, (axis, count, me) in enumerate(axes):
        wide[place] = total
        landing = (from_grid, from_band)[place]
        copies = []
        for step in range(1, count):
            copy = pltpu.make_async_remote_copy(
                src_ref=wide.at[place],
                dst_ref=landing.at[step],
                send_sem=sems.at[place, 0, step],
                recv_sem=sems.at[place, 1, step],
                device_id={axis: lax.rem(me + step, count)},
                device_id_type=MESH,
            )
            copy.start()
            copies.append(copy)
        for step, copy in enumerate(copies):
            copy.wait()
            total = total + landing[step + 1]
    out_ref[...] = total


def summed(table):
    n, bands = lax.axis_size("grid"), lax.axis_size("band")
    tile = (-(-table.shape[0] // 8) * 8, 128)
    vmem = pl.BlockSpec(memory_space=pltpu.VMEM)
    padded = jnp.pad(
        table, ((0, tile[0] - table.shape[0]), (0, tile[1] - table.shape[1]))
    )
    result = pl.pallas_call(
        functools.partial(sum_kernel, n, bands),
        out_shape=jax.ShapeDtypeStruct(tile, jnp.float32),
        in_specs=[vmem],
        out_specs=vmem,
        scratch_shapes=[
            pltpu.VMEM((2,) + tile, jnp.float32),
            pltpu.VMEM((n,) + tile, jnp.float32),
            pltpu.VMEM((bands,) + tile, jnp.float32),
            pltpu.SemaphoreType.DMA((2, 2, max(n, bands))),
        ],
        compiler_params=pltpu.CompilerParams(collective_id=1, has_side_effects=True),
    )(padded)
    return result[: table.shape[0], : table.shape[1]]


def transform_kernel(
    n, halves, chunks, chips,
    mix_ref, share_ref, orbital_ref, kern_ref, fwd_ref, bwd_ref,
    own_ref, term_ref,
    send_one, recv_one, send_two, recv_two, second_ref, off_ref, twin_ref, going, coming, every_ref,
    sems_one_send, sems_one_recv, sems_two_send, sems_two_recv, sems_own, sems_twin, sems_chip, sems_in, sems_keep,
):
    bands = every_ref.shape[0]
    planes, length = own_ref.shape[0], own_ref.shape[2]
    band_me = lax.axis_index("band")
    chip, core = band_me // 2, lax.rem(band_me, 2)
    partner = chip * 2 + 1 - core
    peers = [lax.rem(chip + step, chips) * 2 + core for step in range(1, chips)]
    depth = length // n
    rows = depth // halves
    chunk = planes // chunks
    me = lax.axis_index("grid")
    barrier = pltpu.get_barrier_semaphore()
    for step in range(1, n):
        pl.semaphore_signal(
            barrier, inc=1, device_id={"grid": lax.rem(me + step, n)}, device_id_type=MESH
        )
    for peer in [partner] + peers:
        pl.semaphore_signal(barrier, inc=1, device_id={"band": peer}, device_id_type=MESH)
    pl.semaphore_wait(barrier, n - 1 + chips)

    def part_copy(source, band, part, slot, target):
        place = pl.ds(part * chunk, chunk)
        return pltpu.make_async_remote_copy(
            src_ref=source.at[place],
            dst_ref=every_ref.at[band, place],
            send_sem=sems_in.at[0, part, slot],
            recv_sem=sems_in.at[1, part, slot],
            device_id={"band": target},
            device_id_type=MESH,
        )

    def direct_copies(part):
        return [
            part_copy(orbital_ref, band_me, part, slot, target)
            for slot, target in enumerate(peers + [partner])
        ]

    def passed_copies(part):
        copies = []
        for step in range(1, chips):
            band = lax.rem(chip + chips - step, chips) * 2 + core
            copies.append(part_copy(every_ref.at[band], band, part, chips - 1 + step, partner))
        return copies

    keep = pltpu.make_async_copy(orbital_ref, every_ref.at[band_me], sems_keep.at[0])
    keep.start()
    for part in range(min(2, chunks)):
        for copy in direct_copies(part):
            copy.start()
    keep.wait()

    def out_copies(part, half):
        size = chunk * rows
        mine = pl.ds(pl.multiple_of(me * (planes * rows) + part * size, size), size)
        copies = []
        for step in range(1, n):
            target = lax.rem(me + step, n)
            copies.append(
                pltpu.make_async_remote_copy(
                    src_ref=send_one.at[target, half, :, pl.ds(part * size, size), :],
                    dst_ref=recv_one.at[half, :, mine, :],
                    send_sem=sems_one_send.at[part, half, step],
                    recv_sem=sems_one_recv.at[part, half, step],
                    device_id={"grid": target},
                    device_id_type=MESH,
                )
            )
        return copies

    def own_copy(half):
        size = planes * rows
        return pltpu.make_async_copy(
            send_one.at[me, half],
            recv_one.at[half, :, pl.ds(pl.multiple_of(me * size, size), size), :],
            sems_own.at[half],
        )

    def back_copies(half, part):
        size = planes * rows
        step_size = chunk * rows
        copies = []
        for step in range(1, n):
            target = lax.rem(me + step, n)
            start = pl.multiple_of(target * size + part * step_size, step_size)
            copies.append(
                pltpu.make_async_remote_copy(
                    src_ref=send_two.at[half, :, pl.ds(start, step_size), :],
                    dst_ref=recv_two.at[half, me, :, pl.ds(part * step_size, step_size), :],
                    send_sem=sems_two_send.at[part, half, step],
                    recv_sem=sems_two_recv.at[part, half, step],
                    device_id={"grid": target},
                    device_id_type=MESH,
                )
            )
        return copies

    def own_back(half):
        size = planes * rows
        return pltpu.make_async_copy(
            send_two.at[half, :, pl.ds(pl.multiple_of(me * size, size), size), :],
            recv_two.at[half, me],
            sems_own.at[halves + half],
        )

    def ahead(pair, carry):
        pieces = []
        for which in range(2):
            plane = pair * 2 + which
            values = [every_ref[band, plane] for band in range(bands)]
            own, first, second = [
                sum(mix_ref[kind, band] * values[band] for band in range(1, bands))
                + mix_ref[kind, 0] * values[0]
                for kind in range(3)
            ]
            own_ref[plane] = own
            second_ref[plane] = second
            both = jnp.concatenate([own * own, first * second], axis=1)
            spectrum = times(both, fwd_ref[...])
            pieces.append(
                jnp.concatenate([spectrum[:, :length], spectrum[:, length:]], axis=0)
            )
        result = times(bwd_ref[...], jnp.concatenate(pieces, axis=1))
        for which in range(2):
            for target in range(n):
                for half in range(halves):
                    for part in range(2):
                        low = part * length + target * depth + half * rows
                        send_one[target, half, part, pl.ds((pair * 2 + which) * rows, rows), :] = (
                            result[low : low + rows, which * length : (which + 1) * length]
                        )
        return carry

    for part in range(chunks):
        for copy in direct_copies(part):
            copy.wait_recv()
        for copy in passed_copies(part):
            copy.start()
        if part + 2 < chunks:
            for copy in direct_copies(part + 2):
                copy.start()
        for copy in passed_copies(part):
            copy.wait_recv()
        lax.fori_loop(part * chunk // 2, (part + 1) * chunk // 2, ahead, 0)
        for copy in out_copies(part, 0):
            copy.start()
    for half in range(1, halves):
        for part in range(chunks):
            for copy in out_copies(part, half - 1):
                copy.wait_send()
            for copy in out_copies(part, half):
                copy.start()
    for half in range(halves):
        own_copy(half).start()

    for half in range(halves):
        own_copy(half).wait()
        for part in range(chunks):
            for copy in out_copies(part, half):
                copy.wait_recv()

        def columns(pair, carry):
            pieces = []
            for which in range(2):
                place = pl.ds(pair * 2 + which, length, stride=rows)
                pieces.append(
                    jnp.concatenate(
                        [recv_one[half, 0, place, :], recv_one[half, 1, place, :]], axis=0
                    )
                )
            spectrum = times(bwd_ref[...], jnp.concatenate(pieces, axis=1))
            weights = jnp.concatenate(
                [kern_ref[half * rows + pair * 2], kern_ref[half * rows + pair * 2 + 1]], axis=1
            )
            spectrum = spectrum * jnp.concatenate([weights, weights], axis=0)
            result = times(fwd_ref[...], spectrum)
            for which in range(2):
                place = pl.ds(pair * 2 + which, length, stride=rows)
                lanes = slice(which * length, (which + 1) * length)
                send_two[half, 0, place, :] = result[:length, lanes]
                send_two[half, 1, place, :] = result[length:, lanes]
            return carry

        lax.fori_loop(0, rows // 2, columns, 0)
        own_back(half).start()
        if half < halves - 1:
            for part in range(chunks):
                for copy in back_copies(half, part):
                    copy.start()
    for half in range(halves - 1):
        for part in range(chunks):
            for copy in back_copies(half, part):
                copy.wait_send()
            if half == halves - 2 and part >= chunks - min(2, chunks):
                for copy in back_copies(halves - 1, part - chunks + min(2, chunks)):
                    copy.start()
    if halves == 1:
        for part in range(min(2, chunks)):
            for copy in back_copies(0, part):
                copy.start()

    for half in range(halves):
        own_back(half).wait()

    def twin_copy(part):
        place = pl.ds(part * chunk, chunk)
        return pltpu.make_async_remote_copy(
            src_ref=off_ref.at[place],
            dst_ref=twin_ref.at[place],
            send_sem=sems_twin.at[0, part],
            recv_sem=sems_twin.at[1, part],
            device_id={"band": partner},
            device_id_type=MESH,
        )

    def chip_copies(part):
        place = pl.ds(part * chunk, chunk)
        return [
            pltpu.make_async_remote_copy(
                src_ref=going.at[step, place],
                dst_ref=coming.at[step, place],
                send_sem=sems_chip.at[0, part, step],
                recv_sem=sems_chip.at[1, part, step],
                device_id={"band": peer},
                device_id_type=MESH,
            )
            for step, peer in enumerate(peers)
        ]

    def shared(part):
        twin_copy(part).wait_recv()

        def one(plane, carry):
            mine, other = off_ref[plane], twin_ref[plane]
            for step, peer in enumerate(peers):
                going[step, plane] = (
                    share_ref[band_me, peer] * mine + share_ref[partner, peer] * other
                )
            term_ref[plane] = (
                term_ref[plane]
                + share_ref[band_me, band_me] * mine
                + share_ref[partner, band_me] * other
            )
            return carry

        lax.fori_loop(part * chunk, (part + 1) * chunk, one, 0)
        for copy in chip_copies(part):
            copy.start()

    def home(pair, carry):
        pieces = []
        for which in range(2):
            place = pl.ds((pair * 2 + which) * rows, rows)
            pieces.append(
                jnp.concatenate(
                    [
                        recv_two[half, source, part, place, :]
                        for part in range(2)
                        for source in range(n)
                        for half in range(halves)
                    ],
                    axis=0,
                )
            )
        result = times(fwd_ref[...], jnp.concatenate(pieces, axis=1))
        for which in range(2):
            plane = pair * 2 + which
            lanes = slice(which * length, (which + 1) * length)
            both = jnp.concatenate([result[:length, lanes], result[length:, lanes]], axis=1)
            potential = times(both, bwd_ref[...])
            term_ref[plane] = potential[:, :length] * own_ref[plane]
            off_ref[plane] = potential[:, length:] * second_ref[plane]
        return carry

    for part in range(chunks):
        for copy in back_copies(halves - 1, part):
            copy.wait_send()
        if part + 2 < chunks:
            for copy in back_copies(halves - 1, part + 2):
                copy.start()
        for half in range(halves):
            for copy in back_copies(half, part):
                copy.wait_recv()
        lax.fori_loop(part * chunk // 2, (part + 1) * chunk // 2, home, 0)
        twin_copy(part).start()
        if part > 0:
            shared(part - 1)
    shared(chunks - 1)

    def last(plane, carry):
        total = term_ref[plane]
        for step in range(chips - 1):
            total = total + coming[step, plane]
        term_ref[plane] = total
        return carry

    for part in range(chunks):
        for copy in chip_copies(part):
            copy.wait()
        lax.fori_loop(part * chunk, (part + 1) * chunk, last, 0)
        twin_copy(part).wait_send()
    for part in range(chunks):
        for copy in out_copies(part, halves - 1):
            copy.wait_send()
        for copy in direct_copies(part) + passed_copies(part):
            copy.wait_send()


def exchanged(mix, share, orbital, kernel):
    n = lax.axis_size("grid")
    planes, length = orbital.shape[0], orbital.shape[2]
    chips = lax.axis_size("band") // 2
    depth = length // n
    halves = 2 if depth % 16 == 0 else 1
    rows = depth // halves
    chunk = max(planes // 4, 2)
    chunks = planes // chunk
    forward = complex_table(length)
    vmem = pl.BlockSpec(memory_space=pltpu.VMEM)
    smem = pl.BlockSpec(memory_space=pltpu.SMEM)
    slab = jax.ShapeDtypeStruct(orbital.shape, jnp.float32)
    block = planes * rows
    return pl.pallas_call(
        functools.partial(transform_kernel, n, halves, chunks, chips),
        out_shape=(slab, slab),
        in_specs=[smem] * 2 + [vmem] * 4,
        out_specs=(vmem, vmem),
        scratch_shapes=[
            pltpu.VMEM((n, halves, 2, block, length), jnp.float32),
            pltpu.VMEM((halves, 2, n * block, length), jnp.float32),
            pltpu.VMEM((halves, 2, n * block, length), jnp.float32),
            pltpu.VMEM((halves, n, 2, block, length), jnp.float32),
            pltpu.VMEM(slab.shape, jnp.float32),
            pltpu.VMEM(slab.shape, jnp.float32),
            pltpu.VMEM(slab.shape, jnp.float32),
            pltpu.VMEM((chips - 1,) + slab.shape, jnp.float32),
            pltpu.VMEM((chips - 1,) + slab.shape, jnp.float32),
            pltpu.VMEM((2 * chips,) + slab.shape, jnp.float32),
            pltpu.SemaphoreType.DMA((chunks, halves, n)),
            pltpu.SemaphoreType.DMA((chunks, halves, n)),
            pltpu.SemaphoreType.DMA((chunks, halves, n)),
            pltpu.SemaphoreType.DMA((chunks, halves, n)),
            pltpu.SemaphoreType.DMA((2 * halves,)),
            pltpu.SemaphoreType.DMA((2, chunks)),
            pltpu.SemaphoreType.DMA((2, chunks, max(chips - 1, 1))),
            pltpu.SemaphoreType.DMA((2, chunks, 2 * chips - 1)),
            pltpu.SemaphoreType.DMA((1,)),
        ],
        compiler_params=pltpu.CompilerParams(
            collective_id=0, has_side_effects=True, vmem_limit_bytes=40 * 1024 * 1024
        ),
    )(mix, share, orbital, kernel, jnp.asarray(forward), jnp.asarray(forward.T.copy()))


def assignment(pattern):
    blocks = pattern.shape[0]
    ids = jnp.arange(blocks, dtype=jnp.int32)
    off = ((pattern == 1) & (ids[:, None] != ids[None, :])).astype(jnp.int32).reshape(-1)
    order = jnp.arange(blocks * blocks, dtype=jnp.int32)
    before = jnp.sum(jnp.where(order[None, :] < order[:, None], off[None, :], 0), axis=1)
    chosen = (off[None, :] == 1) & (before[None, :] == ids[:, None])
    chosen = chosen.reshape(blocks, blocks, blocks)
    firsts = jnp.any(chosen, axis=2).astype(jnp.float32)
    seconds = jnp.any(chosen, axis=1).astype(jnp.float32)
    return firsts, seconds


def local(orbitals, pivots, pattern):
    slab_planes = orbitals.shape[1]
    length = orbitals.shape[3]
    block_total = pattern.shape[0]
    grid_index = lax.axis_index("grid")
    band_index = lax.axis_index("band")
    local_cell = pivots - grid_index * (slab_planes * length * length)
    inside = (local_cell >= 0) & (local_cell < slab_planes * length * length)
    cell = jnp.clip(local_cell, 0, slab_planes * length * length - 1)
    rows = jnp.take(orbitals.reshape(slab_planes * length, length), cell // length, axis=0)
    lanes = jnp.arange(length, dtype=jnp.int32)
    sampled = jnp.sum(jnp.where(lanes[None, :] == (cell % length)[:, None], rows, 0.0), axis=1)
    own = jnp.where(inside, sampled, 0.0)
    ids = jnp.arange(block_total, dtype=jnp.int32)
    picked = summed(jnp.where(ids[:, None] == band_index, own[None, :], 0.0))
    gram_matrix = jnp.dot(picked.T, picked, precision=precise)
    factor = jnp.linalg.cholesky(gram_matrix)
    rotation = lax.linalg.triangular_solve(factor, picked.T, left_side=True, lower=True).T
    firsts, seconds = assignment(pattern)
    selectors = jnp.stack(
        [
            (ids == band_index).astype(jnp.float32),
            lax.dynamic_index_in_dim(firsts, band_index, 0, keepdims=False),
            lax.dynamic_index_in_dim(seconds, band_index, 0, keepdims=False),
        ]
    )
    coefficients = jnp.dot(selectors, rotation.T, precision=precise)
    depth = length // lax.axis_size("grid")
    kernel = coulomb(length, grid_index * depth, depth)
    localized, exchange_term = exchanged(coefficients, firsts, orbitals[0], kernel)
    return (localized[None], exchange_term[None])


def solution(mesh):
    return jax.shard_map(
        local,
        mesh=mesh,
        in_specs=(P("band", "grid", None, None), P(), P()),
        out_specs=(P("band", "grid", None, None), P("band", "grid", None, None)),
        check_vma=False,
    )
```

```python
import functools

import jax
import jax.numpy as jnp
import numpy as np
from jax import lax
from jax.experimental import pallas as pl
from jax.experimental.pallas import tpu as pltpu
from jax.sharding import PartitionSpec as P

precise = lax.Precision.HIGHEST
MESH = pl.DeviceIdType.MESH


def hartley_tables(length):
    across = np.arange(length)
    angles = (across[:, None] * across[None, :] % length) * (2.0 * np.pi / length)
    table = np.cos(angles) + np.sin(angles)
    high = table.astype(jnp.bfloat16)
    low = (table - high.astype(np.float64)).astype(jnp.bfloat16)
    right = np.block([[high, low], [high, low]])
    return jnp.asarray(right.T.copy()), jnp.asarray(right)


def in_two(values, axis):
    high = values.astype(jnp.bfloat16)
    low = (values - high.astype(jnp.float32)).astype(jnp.bfloat16)
    return jnp.concatenate([high, low], axis=axis)


def along_lanes(values, table):
    length = values.shape[1]
    both = jnp.dot(in_two(values, 1), table, preferred_element_type=jnp.float32)
    return both[:, :length] + both[:, length:]


def along_rows(values, table):
    length = values.shape[0]
    both = jnp.dot(table, in_two(values, 0), preferred_element_type=jnp.float32)
    return both[:length] + both[length:]


def wrapped(indices, length):
    return jnp.where(indices < length // 2, indices, indices - length)


def coulomb(length, row_start, row_count):
    wave = wrapped(jnp.arange(length, dtype=jnp.int32), length).astype(jnp.float32)
    rows = wrapped(row_start + jnp.arange(row_count, dtype=jnp.int32), length).astype(jnp.float32)
    squared = rows[:, None, None] ** 2 + wave[None, :, None] ** 2 + wave[None, None, :] ** 2
    scaling = float(length) ** 1.5
    return jnp.where(squared > 0, 0.25 / (scaling * jnp.maximum(squared, 1.0)), 0.0)


def sum_kernel(n, bands, own_ref, out_ref, wide, from_grid, from_band, sems):
    grid_me, band_me = lax.axis_index("grid"), lax.axis_index("band")
    barrier = pltpu.get_barrier_semaphore()
    axes = (("grid", n, grid_me), ("band", bands, band_me))
    for axis, count, me in axes:
        for step in range(1, count):
            pl.semaphore_signal(
                barrier, inc=1, device_id={axis: lax.rem(me + step, count)}, device_id_type=MESH
            )
    pl.semaphore_wait(barrier, n + bands - 2)
    total = own_ref[...]
    for place, (axis, count, me) in enumerate(axes):
        wide[place] = total
        landing = (from_grid, from_band)[place]
        copies = []
        for step in range(1, count):
            copy = pltpu.make_async_remote_copy(
                src_ref=wide.at[place],
                dst_ref=landing.at[step],
                send_sem=sems.at[place, 0, step],
                recv_sem=sems.at[place, 1, step],
                device_id={axis: lax.rem(me + step, count)},
                device_id_type=MESH,
            )
            copy.start()
            copies.append(copy)
        for step, copy in enumerate(copies):
            copy.wait()
            total = total + landing[step + 1]
    out_ref[...] = total


def summed(table):
    n, bands = lax.axis_size("grid"), lax.axis_size("band")
    tile = (-(-table.shape[0] // 8) * 8, 128)
    vmem = pl.BlockSpec(memory_space=pltpu.VMEM)
    padded = jnp.pad(
        table, ((0, tile[0] - table.shape[0]), (0, tile[1] - table.shape[1]))
    )
    result = pl.pallas_call(
        functools.partial(sum_kernel, n, bands),
        out_shape=jax.ShapeDtypeStruct(tile, jnp.float32),
        in_specs=[vmem],
        out_specs=vmem,
        scratch_shapes=[
            pltpu.VMEM((2,) + tile, jnp.float32),
            pltpu.VMEM((n,) + tile, jnp.float32),
            pltpu.VMEM((bands,) + tile, jnp.float32),
            pltpu.SemaphoreType.DMA((2, 2, max(n, bands))),
        ],
        compiler_params=pltpu.CompilerParams(collective_id=1, has_side_effects=True),
    )(padded)
    return result[: table.shape[0], : table.shape[1]]


def transform_kernel(
    n, halves, chunks, chips,
    mix_ref, share_ref, orbital_ref, kern_ref, left_ref, right_ref,
    own_ref, term_ref,
    send_one, recv_one, send_two, recv_two, second_ref, off_ref, twin_ref, going, coming, every_ref,
    sems_one_send, sems_one_recv, sems_two_send, sems_two_recv, sems_own, sems_twin, sems_chip, sems_in, sems_keep,
):
    bands = every_ref.shape[0]
    planes, length = own_ref.shape[0], own_ref.shape[2]
    band_me = lax.axis_index("band")
    chip, core = band_me // 2, lax.rem(band_me, 2)
    partner = chip * 2 + 1 - core
    peers = [lax.rem(chip + step, chips) * 2 + core for step in range(1, chips)]
    depth = length // n
    rows = depth // halves
    chunk = planes // chunks
    me = lax.axis_index("grid")
    barrier = pltpu.get_barrier_semaphore()
    for step in range(1, n):
        pl.semaphore_signal(
            barrier, inc=1, device_id={"grid": lax.rem(me + step, n)}, device_id_type=MESH
        )
    for peer in [partner] + peers:
        pl.semaphore_signal(barrier, inc=1, device_id={"band": peer}, device_id_type=MESH)
    pl.semaphore_wait(barrier, n - 1 + chips)

    def part_copy(source, band, part, slot, target):
        place = pl.ds(part * chunk, chunk)
        return pltpu.make_async_remote_copy(
            src_ref=source.at[place],
            dst_ref=every_ref.at[band, place],
            send_sem=sems_in.at[0, part, slot],
            recv_sem=sems_in.at[1, part, slot],
            device_id={"band": target},
            device_id_type=MESH,
        )

    def direct_copies(part):
        return [
            part_copy(orbital_ref, band_me, part, slot, target)
            for slot, target in enumerate(peers + [partner])
        ]

    def passed_copies(part):
        copies = []
        for step in range(1, chips):
            band = lax.rem(chip + chips - step, chips) * 2 + core
            copies.append(part_copy(every_ref.at[band], band, part, chips - 1 + step, partner))
        return copies

    keep = pltpu.make_async_copy(orbital_ref, every_ref.at[band_me], sems_keep.at[0])
    keep.start()
    for part in range(min(2, chunks)):
        for copy in direct_copies(part):
            copy.start()
    keep.wait()

    def out_copies(part, half):
        size = chunk * rows
        mine = pl.ds(pl.multiple_of(me * (planes * rows) + part * size, size), size)
        copies = []
        for step in range(1, n):
            target = lax.rem(me + step, n)
            copies.append(
                pltpu.make_async_remote_copy(
                    src_ref=send_one.at[target, half, :, pl.ds(part * size, size), :],
                    dst_ref=recv_one.at[half, :, mine, :],
                    send_sem=sems_one_send.at[part, half, step],
                    recv_sem=sems_one_recv.at[part, half, step],
                    device_id={"grid": target},
                    device_id_type=MESH,
                )
            )
        return copies

    def own_copy(half):
        size = planes * rows
        return pltpu.make_async_copy(
            send_one.at[me, half],
            recv_one.at[half, :, pl.ds(pl.multiple_of(me * size, size), size), :],
            sems_own.at[half],
        )

    def back_copies(half, part):
        size = planes * rows
        step_size = chunk * rows
        copies = []
        for step in range(1, n):
            target = lax.rem(me + step, n)
            start = pl.multiple_of(target * size + part * step_size, step_size)
            copies.append(
                pltpu.make_async_remote_copy(
                    src_ref=send_two.at[half, :, pl.ds(start, step_size), :],
                    dst_ref=recv_two.at[half, me, :, pl.ds(part * step_size, step_size), :],
                    send_sem=sems_two_send.at[part, half, step],
                    recv_sem=sems_two_recv.at[part, half, step],
                    device_id={"grid": target},
                    device_id_type=MESH,
                )
            )
        return copies

    def own_back(half):
        size = planes * rows
        return pltpu.make_async_copy(
            send_two.at[half, :, pl.ds(pl.multiple_of(me * size, size), size), :],
            recv_two.at[half, me],
            sems_own.at[halves + half],
        )

    def ahead(pair, carry):
        for which in range(2):
            plane = pair * 2 + which
            values = [every_ref[band, plane] for band in range(bands)]
            own, first, second = [
                sum(mix_ref[kind, band] * values[band] for band in range(1, bands))
                + mix_ref[kind, 0] * values[0]
                for kind in range(3)
            ]
            own_ref[plane] = own
            second_ref[plane] = second
            both = jnp.concatenate([own * own, first * second], axis=0)
            spectrum = along_lanes(both, right_ref[...])
            result = along_rows(
                jnp.concatenate([spectrum[:length], spectrum[length:]], axis=1), left_ref[...]
            )
            for target in range(n):
                for half in range(halves):
                    for part in range(2):
                        low = target * depth + half * rows
                        send_one[target, half, part, pl.ds(plane * rows, rows), :] = (
                            result[low : low + rows, part * length : (part + 1) * length]
                        )
        return carry

    for part in range(chunks):
        for copy in direct_copies(part):
            copy.wait_recv()
        for copy in passed_copies(part):
            copy.start()
        if part + 2 < chunks:
            for copy in direct_copies(part + 2):
                copy.start()
        for copy in passed_copies(part):
            copy.wait_recv()
        lax.fori_loop(part * chunk // 2, (part + 1) * chunk // 2, ahead, 0)
        for copy in out_copies(part, 0):
            copy.start()
    for half in range(1, halves):
        for part in range(chunks):
            for copy in out_copies(part, half - 1):
                copy.wait_send()
            for copy in out_copies(part, half):
                copy.start()
    for half in range(halves):
        own_copy(half).start()

    for half in range(halves):
        own_copy(half).wait()
        for part in range(chunks):
            for copy in out_copies(part, half):
                copy.wait_recv()

        def columns(pair, carry):
            for which in range(2):
                row = pair * 2 + which
                place = pl.ds(row, length, stride=rows)
                both = jnp.concatenate(
                    [recv_one[half, 0, place, :], recv_one[half, 1, place, :]], axis=1
                )
                weights = kern_ref[half * rows + row]
                spectrum = along_rows(both, left_ref[...])
                spectrum = spectrum * jnp.concatenate([weights, weights], axis=1)
                result = along_rows(spectrum, left_ref[...])
                send_two[half, 0, place, :] = result[:, :length]
                send_two[half, 1, place, :] = result[:, length:]
            return carry

        lax.fori_loop(0, rows // 2, columns, 0)
        own_back(half).start()
        if half < halves - 1:
            for part in range(chunks):
                for copy in back_copies(half, part):
                    copy.start()
    for half in range(halves - 1):
        for part in range(chunks):
            for copy in back_copies(half, part):
                copy.wait_send()
            if half == halves - 2 and part >= chunks - min(2, chunks):
                for copy in back_copies(halves - 1, part - chunks + min(2, chunks)):
                    copy.start()
    if halves == 1:
        for part in range(min(2, chunks)):
            for copy in back_copies(0, part):
                copy.start()

    for half in range(halves):
        own_back(half).wait()

    def twin_copy(part):
        place = pl.ds(part * chunk, chunk)
        return pltpu.make_async_remote_copy(
            src_ref=off_ref.at[place],
            dst_ref=twin_ref.at[place],
            send_sem=sems_twin.at[0, part],
            recv_sem=sems_twin.at[1, part],
            device_id={"band": partner},
            device_id_type=MESH,
        )

    def chip_copies(part):
        place = pl.ds(part * chunk, chunk)
        return [
            pltpu.make_async_remote_copy(
                src_ref=going.at[step, place],
                dst_ref=coming.at[step, place],
                send_sem=sems_chip.at[0, part, step],
                recv_sem=sems_chip.at[1, part, step],
                device_id={"band": peer},
                device_id_type=MESH,
            )
            for step, peer in enumerate(peers)
        ]

    def shared(part):
        twin_copy(part).wait_recv()

        def one(plane, carry):
            mine, other = off_ref[plane], twin_ref[plane]
            for step, peer in enumerate(peers):
                going[step, plane] = (
                    share_ref[band_me, peer] * mine + share_ref[partner, peer] * other
                )
            term_ref[plane] = (
                term_ref[plane]
                + share_ref[band_me, band_me] * mine
                + share_ref[partner, band_me] * other
            )
            return carry

        lax.fori_loop(part * chunk, (part + 1) * chunk, one, 0)
        for copy in chip_copies(part):
            copy.start()

    def home(pair, carry):
        for which in range(2):
            plane = pair * 2 + which
            place = pl.ds(plane * rows, rows)
            both = jnp.concatenate(
                [
                    jnp.concatenate(
                        [
                            recv_two[half, source, part, place, :]
                            for source in range(n)
                            for half in range(halves)
                        ],
                        axis=0,
                    )
                    for part in range(2)
                ],
                axis=1,
            )
            result = along_rows(both, left_ref[...])
            potential = along_lanes(
                jnp.concatenate([result[:, :length], result[:, length:]], axis=0), right_ref[...]
            )
            term_ref[plane] = potential[:length] * own_ref[plane]
            off_ref[plane] = potential[length:] * second_ref[plane]
        return carry

    for part in range(chunks):
        for copy in back_copies(halves - 1, part):
            copy.wait_send()
        if part + 2 < chunks:
            for copy in back_copies(halves - 1, part + 2):
                copy.start()
        for half in range(halves):
            for copy in back_copies(half, part):
                copy.wait_recv()
        lax.fori_loop(part * chunk // 2, (part + 1) * chunk // 2, home, 0)
        twin_copy(part).start()
        if part > 0:
            shared(part - 1)
    shared(chunks - 1)

    def last(plane, carry):
        total = term_ref[plane]
        for step in range(chips - 1):
            total = total + coming[step, plane]
        term_ref[plane] = total
        return carry

    for part in range(chunks):
        for copy in chip_copies(part):
            copy.wait()
        lax.fori_loop(part * chunk, (part + 1) * chunk, last, 0)
        twin_copy(part).wait_send()
    for part in range(chunks):
        for copy in out_copies(part, halves - 1):
            copy.wait_send()
        for copy in direct_copies(part) + passed_copies(part):
            copy.wait_send()


def exchanged(mix, share, orbital, kernel):
    n = lax.axis_size("grid")
    planes, length = orbital.shape[0], orbital.shape[2]
    chips = lax.axis_size("band") // 2
    depth = length // n
    halves = 2 if depth % 16 == 0 else 1
    rows = depth // halves
    chunk = max(planes // 4, 2)
    chunks = planes // chunk
    left, right = hartley_tables(length)
    vmem = pl.BlockSpec(memory_space=pltpu.VMEM)
    smem = pl.BlockSpec(memory_space=pltpu.SMEM)
    slab = jax.ShapeDtypeStruct(orbital.shape, jnp.float32)
    block = planes * rows
    return pl.pallas_call(
        functools.partial(transform_kernel, n, halves, chunks, chips),
        out_shape=(slab, slab),
        in_specs=[smem] * 2 + [vmem] * 4,
        out_specs=(vmem, vmem),
        scratch_shapes=[
            pltpu.VMEM((n, halves, 2, block, length), jnp.float32),
            pltpu.VMEM((halves, 2, n * block, length), jnp.float32),
            pltpu.VMEM((halves, 2, n * block, length), jnp.float32),
            pltpu.VMEM((halves, n, 2, block, length), jnp.float32),
            pltpu.VMEM(slab.shape, jnp.float32),
            pltpu.VMEM(slab.shape, jnp.float32),
            pltpu.VMEM(slab.shape, jnp.float32),
            pltpu.VMEM((chips - 1,) + slab.shape, jnp.float32),
            pltpu.VMEM((chips - 1,) + slab.shape, jnp.float32),
            pltpu.VMEM((2 * chips,) + slab.shape, jnp.float32),
            pltpu.SemaphoreType.DMA((chunks, halves, n)),
            pltpu.SemaphoreType.DMA((chunks, halves, n)),
            pltpu.SemaphoreType.DMA((chunks, halves, n)),
            pltpu.SemaphoreType.DMA((chunks, halves, n)),
            pltpu.SemaphoreType.DMA((2 * halves,)),
            pltpu.SemaphoreType.DMA((2, chunks)),
            pltpu.SemaphoreType.DMA((2, chunks, max(chips - 1, 1))),
            pltpu.SemaphoreType.DMA((2, chunks, 2 * chips - 1)),
            pltpu.SemaphoreType.DMA((1,)),
        ],
        compiler_params=pltpu.CompilerParams(
            collective_id=0, has_side_effects=True, vmem_limit_bytes=40 * 1024 * 1024
        ),
    )(mix, share, orbital, kernel, left, right)


def assignment(pattern):
    blocks = pattern.shape[0]
    ids = jnp.arange(blocks, dtype=jnp.int32)
    off = ((pattern == 1) & (ids[:, None] != ids[None, :])).astype(jnp.int32).reshape(-1)
    order = jnp.arange(blocks * blocks, dtype=jnp.int32)
    before = jnp.sum(jnp.where(order[None, :] < order[:, None], off[None, :], 0), axis=1)
    chosen = (off[None, :] == 1) & (before[None, :] == ids[:, None])
    chosen = chosen.reshape(blocks, blocks, blocks)
    firsts = jnp.any(chosen, axis=2).astype(jnp.float32)
    seconds = jnp.any(chosen, axis=1).astype(jnp.float32)
    return firsts, seconds


def local(orbitals, pivots, pattern):
    slab_planes = orbitals.shape[1]
    length = orbitals.shape[3]
    block_total = pattern.shape[0]
    grid_index = lax.axis_index("grid")
    band_index = lax.axis_index("band")
    local_cell = pivots - grid_index * (slab_planes * length * length)
    inside = (local_cell >= 0) & (local_cell < slab_planes * length * length)
    cell = jnp.clip(local_cell, 0, slab_planes * length * length - 1)
    rows = jnp.take(orbitals.reshape(slab_planes * length, length), cell // length, axis=0)
    lanes = jnp.arange(length, dtype=jnp.int32)
    sampled = jnp.sum(jnp.where(lanes[None, :] == (cell % length)[:, None], rows, 0.0), axis=1)
    own = jnp.where(inside, sampled, 0.0)
    ids = jnp.arange(block_total, dtype=jnp.int32)
    picked = summed(jnp.where(ids[:, None] == band_index, own[None, :], 0.0))
    gram_matrix = jnp.dot(picked.T, picked, precision=precise)
    factor = jnp.linalg.cholesky(gram_matrix)
    rotation = lax.linalg.triangular_solve(factor, picked.T, left_side=True, lower=True).T
    firsts, seconds = assignment(pattern)
    selectors = jnp.stack(
        [
            (ids == band_index).astype(jnp.float32),
            lax.dynamic_index_in_dim(firsts, band_index, 0, keepdims=False),
            lax.dynamic_index_in_dim(seconds, band_index, 0, keepdims=False),
        ]
    )
    coefficients = jnp.dot(selectors, rotation.T, precision=precise)
    depth = length // lax.axis_size("grid")
    kernel = coulomb(length, grid_index * depth, depth)
    localized, exchange_term = exchanged(coefficients, firsts, orbitals[0], kernel)
    return (localized[None], exchange_term[None])


def solution(mesh):
    return jax.shard_map(
        local,
        mesh=mesh,
        in_specs=(P("band", "grid", None, None), P(), P()),
        out_specs=(P("band", "grid", None, None), P("band", "grid", None, None)),
        check_vma=False,
    )
```

```python
import functools

import jax
import jax.numpy as jnp
import numpy as np
from jax import lax
from jax.experimental import pallas as pl
from jax.experimental.pallas import tpu as pltpu
from jax.sharding import PartitionSpec as P

MESH = pl.DeviceIdType.MESH


def hartley_tables(length):
    across = np.arange(length)
    angles = (across[:, None] * across[None, :] % length) * (2.0 * np.pi / length)
    table = np.cos(angles) + np.sin(angles)
    high = table.astype(jnp.bfloat16)
    low = (table - high.astype(np.float64)).astype(jnp.bfloat16)
    right = np.block([[high, low], [high, low]])
    return jnp.asarray(right.T.copy()), jnp.asarray(right)


def in_two(values, axis):
    high = values.astype(jnp.bfloat16)
    low = (values - high.astype(jnp.float32)).astype(jnp.bfloat16)
    return jnp.concatenate([high, low], axis=axis)


def along_lanes(values, table):
    length = values.shape[1]
    both = jnp.dot(in_two(values, 1), table, preferred_element_type=jnp.float32)
    return both[:, :length] + both[:, length:]


def along_rows(values, table):
    length = values.shape[0]
    both = jnp.dot(table, in_two(values, 0), preferred_element_type=jnp.float32)
    return both[:length] + both[length:]


def wrapped(indices, length):
    return jnp.where(indices < length // 2, indices, indices - length).astype(jnp.float32)


def transform_kernel(
    n, halves, ahead_chunks, back_chunks, chips, window, lag,
    pivot_ref, pattern_ref, orbital_ref, left_hbm, right_hbm,
    own_ref, term_ref,
    send_one, recv_one, send_two, recv_two, second_ref, off_ref, twin_ref, going, coming,
    every_ref, raw_ref, left_ref, right_ref, base_ref, picks, from_band, from_grid, mix_ref, share_ref,
    sems_one_send, sems_one_recv, sems_two_send, sems_two_recv, sems_own, sems_twin, sems_chip, sems_in, sems_keep,
    sems_band, sems_grid,
):
    bands = every_ref.shape[0] + 1
    planes, length = own_ref.shape[0], own_ref.shape[2]
    me, band_me = lax.axis_index("grid"), lax.axis_index("band")
    chip, core = band_me // 2, lax.rem(band_me, 2)
    partner = chip * 2 + 1 - core
    peers = [lax.rem(chip + step, chips) * 2 + core for step in range(1, chips)]
    sources = [lax.rem(chip + chips - step, chips) * 2 for step in range(1, chips)]
    slots = [low + core for low in sources] + [partner] + [low + 1 - core for low in sources]
    depth = length // n
    rows = depth // halves
    size = planes * rows
    ahead_chunk, back_chunk = planes // ahead_chunks, planes // back_chunks
    barrier = pltpu.get_barrier_semaphore()
    for axis, count, here in (("grid", n, me), ("band", bands, band_me)):
        for step in range(1, count):
            pl.semaphore_signal(
                barrier, inc=1, device_id={axis: lax.rem(here + step, count)}, device_id_type=MESH
            )
    keep = [
        pltpu.make_async_copy(source, target, sems_keep.at[place])
        for place, (source, target) in enumerate(
            ((orbital_ref, raw_ref), (left_hbm, left_ref), (right_hbm, right_ref))
        )
    ]
    for copy in keep:
        copy.start()

    tile = picks.shape[2:]
    sublane = lax.broadcasted_iota(jnp.int32, tile, 0)
    lane = lax.broadcasted_iota(jnp.int32, tile, 1)
    keep[0].wait()
    slab = planes * length * length
    for column in range(bands):
        cell = pivot_ref[column] - me * slab
        inside = jnp.where((cell >= 0) & (cell < slab), 1, 0)
        cell = jnp.clip(cell, 0, slab - 1)
        row = raw_ref[cell // (length * length), pl.ds(lax.rem(cell // length, length), 1), :]
        mine = (sublane == band_me) & (lane == lax.rem(cell, length)) & (jnp.full(tile, inside) > 0)
        picks[0, column] = jnp.where(mine, jnp.broadcast_to(row, tile), 0.0)
    pl.semaphore_wait(barrier, n + bands - 2)

    def pick_copies(axis, count, here, source, landing, sems):
        return [
            pltpu.make_async_remote_copy(
                src_ref=source,
                dst_ref=landing.at[step - 1],
                send_sem=sems.at[0, step],
                recv_sem=sems.at[1, step],
                device_id={axis: lax.rem(here + step, count)},
                device_id_type=MESH,
            )
            for step in range(1, count)
        ]

    band_picks = pick_copies("band", bands, band_me, picks.at[0], from_band, sems_band)
    grid_picks = pick_copies("grid", n, me, picks.at[1], from_grid, sems_grid)
    for copy in band_picks:
        copy.start()

    def part_copy(source, part, slot, target):
        place = pl.ds(part * ahead_chunk, ahead_chunk)
        return pltpu.make_async_remote_copy(
            src_ref=source.at[place],
            dst_ref=every_ref.at[slot, place],
            send_sem=sems_in.at[0, part, slot],
            recv_sem=sems_in.at[1, part, slot],
            device_id={"band": target},
            device_id_type=MESH,
        )

    def direct_copies(part):
        return [part_copy(raw_ref, part, slot, target) for slot, target in enumerate(peers + [partner])]

    def passed_copies(part):
        return [
            part_copy(every_ref.at[step - 1], part, chips - 1 + step, partner) for step in range(1, chips)
        ]

    for part in range(min(2, ahead_chunks)):
        for copy in direct_copies(part):
            copy.start()

    for copy in band_picks:
        copy.wait()
    total = picks[0]
    for step in range(bands - 1):
        total = total + from_band[step]
    picks[1] = total
    for copy in grid_picks:
        copy.start()

    waves = [wrapped(lax.broadcasted_iota(jnp.int32, (length, length), axis), length) for axis in range(2)]
    base_ref[...] = waves[0] * waves[0] + waves[1] * waves[1]
    firsts = [[0.0] * bands for _ in range(2)]
    seconds = [0.0] * bands
    before = 0
    for row in range(bands):
        for column in range(bands):
            if row != column:
                on = jnp.where(pattern_ref[row, column] == 1, 1, 0)
                for place, band in enumerate((band_me, partner)):
                    chosen = jnp.where((on == 1) & (before == band), 1.0, 0.0)
                    firsts[place][row] = firsts[place][row] + chosen
                    if place == 0:
                        seconds[column] = seconds[column] + chosen
                before = before + on
    for place in range(2):
        for band in range(bands):
            share_ref[place, band] = firsts[place][band]

    for copy in grid_picks:
        copy.wait()
    for step in range(n - 1):
        total = total + from_grid[step]
    columns_of = [
        jnp.broadcast_to(jnp.sum(total[column], axis=1, keepdims=True), tile) for column in range(bands)
    ]
    factor = [[None] * bands for _ in range(bands)]
    solved = []
    for row in range(bands):
        for column in range(row + 1):
            value = jnp.sum(columns_of[row] * columns_of[column], axis=0, keepdims=True)
            for step in range(column):
                value = value - factor[row][step] * factor[column][step]
            factor[row][column] = jnp.sqrt(value) if row == column else value / factor[column][column]
        value = columns_of[row]
        for step in range(row):
            value = value - factor[row][step] * solved[step]
        solved.append(value / factor[row][row])
    owns = [jnp.where(band_me == band, 1.0, 0.0) for band in range(bands)]
    for kind, weights in enumerate((owns, firsts[0], seconds)):
        value = weights[0] * solved[0]
        for band in range(1, bands):
            value = value + weights[band] * solved[band]
        mix_ref[kind] = value
    for copy in keep[1:]:
        copy.wait()

    def out_copies(part, half):
        step_size = ahead_chunk * rows
        mine = pl.ds(pl.multiple_of(me * size + part * step_size, step_size), step_size)
        copies = []
        for step in range(1, n):
            target = lax.rem(me + step, n)
            copies.append(
                pltpu.make_async_remote_copy(
                    src_ref=send_one.at[target, half, :, pl.ds(part * step_size, step_size), :],
                    dst_ref=recv_one.at[half, :, mine, :],
                    send_sem=sems_one_send.at[part, half, step],
                    recv_sem=sems_one_recv.at[part, half, step],
                    device_id={"grid": target},
                    device_id_type=MESH,
                )
            )
        return copies

    def own_copy(half):
        return pltpu.make_async_copy(
            send_one.at[me, half],
            recv_one.at[half, :, pl.ds(pl.multiple_of(me * size, size), size), :],
            sems_own.at[half],
        )

    def back_copies(part, half):
        step_size = back_chunk * rows
        copies = []
        for step in range(1, n):
            target = lax.rem(me + step, n)
            start = pl.multiple_of(target * size + part * step_size, step_size)
            copies.append(
                pltpu.make_async_remote_copy(
                    src_ref=send_two.at[half, :, pl.ds(start, step_size), :],
                    dst_ref=recv_two.at[half, me, :, pl.ds(part * step_size, step_size), :],
                    send_sem=sems_two_send.at[part, half, step],
                    recv_sem=sems_two_recv.at[part, half, step],
                    device_id={"grid": target},
                    device_id_type=MESH,
                )
            )
        return copies

    def own_back(half):
        return pltpu.make_async_copy(
            send_two.at[half, :, pl.ds(pl.multiple_of(me * size, size), size), :],
            recv_two.at[half, me],
            sems_own.at[halves + half],
        )

    def ahead(plane, carry):
        values = [raw_ref[plane]] + [every_ref[slot, plane] for slot in range(bands - 1)]
        parts = []
        for kind in range(3):
            value = mix_ref[kind, pl.ds(band_me, 1), :] * values[0]
            for slot in range(bands - 1):
                value = value + mix_ref[kind, pl.ds(slots[slot], 1), :] * values[slot + 1]
            parts.append(value)
        own, first, second = parts
        own_ref[plane] = own
        second_ref[plane] = second
        both = jnp.concatenate([own * own, first * second], axis=0)
        spectrum = along_lanes(both, right_ref[...])
        result = along_rows(
            jnp.concatenate([spectrum[:length], spectrum[length:]], axis=1), left_ref[...]
        )
        for target in range(n):
            for half in range(halves):
                for part in range(2):
                    low = target * depth + half * rows
                    send_one[target, half, part, pl.ds(plane * rows, rows), :] = (
                        result[low : low + rows, part * length : (part + 1) * length]
                    )
        return carry

    def columns(half):
        def step(row, carry):
            place = pl.ds(row, length, stride=rows)
            both = jnp.concatenate(
                [recv_one[half, 0, place, :], recv_one[half, 1, place, :]], axis=1
            )
            wave = wrapped(me * depth + half * rows + row, length)
            squared = base_ref[...] + wave * wave
            scaling = float(length) ** 1.5
            weights = jnp.where(
                squared > 0, 0.25 / (scaling * jnp.maximum(squared, 1.0)), 0.0
            )
            spectrum = along_rows(both, left_ref[...])
            spectrum = spectrum * jnp.concatenate([weights, weights], axis=1)
            result = along_rows(spectrum, left_ref[...])
            send_two[half, 0, place, :] = result[:, :length]
            send_two[half, 1, place, :] = result[:, length:]
            return carry

        lax.fori_loop(0, rows, step, 0)
        own_back(half).start()

    def twin_copy(part):
        place = pl.ds(part * back_chunk, back_chunk)
        return pltpu.make_async_remote_copy(
            src_ref=off_ref.at[place],
            dst_ref=twin_ref.at[place],
            send_sem=sems_twin.at[0, part],
            recv_sem=sems_twin.at[1, part],
            device_id={"band": partner},
            device_id_type=MESH,
        )

    def chip_copies(part):
        place = pl.ds(part * back_chunk, back_chunk)
        return [
            pltpu.make_async_remote_copy(
                src_ref=going.at[step, place],
                dst_ref=coming.at[step, place],
                send_sem=sems_chip.at[0, part, step],
                recv_sem=sems_chip.at[1, part, step],
                device_id={"band": peer},
                device_id_type=MESH,
            )
            for step, peer in enumerate(peers)
        ]

    def shared(part):
        twin_copy(part).wait_recv()

        def one(plane, carry):
            mine, other = off_ref[plane], twin_ref[plane]
            for step, peer in enumerate(peers):
                going[step, plane] = share_ref[0, peer] * mine + share_ref[1, peer] * other
            term_ref[plane] = (
                term_ref[plane] + share_ref[0, band_me] * mine + share_ref[1, band_me] * other
            )
            return carry

        lax.fori_loop(part * back_chunk, (part + 1) * back_chunk, one, 0)
        for copy in chip_copies(part):
            copy.start()

    def home(plane, carry):
        place = pl.ds(plane * rows, rows)
        both = jnp.concatenate(
            [
                jnp.concatenate(
                    [recv_two[half, source, part, place, :] for source in range(n) for half in range(halves)],
                    axis=0,
                )
                for part in range(2)
            ],
            axis=1,
        )
        result = along_rows(both, left_ref[...])
        potential = along_lanes(
            jnp.concatenate([result[:, :length], result[:, length:]], axis=0), right_ref[...]
        )
        term_ref[plane] = potential[:length] * own_ref[plane]
        off_ref[plane] = potential[length:] * second_ref[plane]
        return carry

    def last(plane, carry):
        total = term_ref[plane]
        for step in range(chips - 1):
            total = total + coming[step, plane]
        term_ref[plane] = total
        return carry

    def copies_of(piece):
        kind, part, half = piece
        return back_copies(part, half) if kind else out_copies(part, half)

    forward, late = [], []
    for part in range(ahead_chunks):
        forward.append((0, part, 0))
        late.extend((0, part, half) for half in range(1, halves))
        if part % 2 == 1 and part < ahead_chunks - 1 and late:
            forward.append(late.pop(0))
    forward = forward + late
    backward = []
    for place in range(back_chunks + lag * (halves - 1)):
        for half in range(halves):
            if 0 <= place - lag * half < back_chunks:
                backward.append((1, place - lag * half, half))
    pieces = forward + backward
    arrived, filtered, finished = set(), set(), set()

    def arrive(piece):
        if piece not in arrived:
            arrived.add(piece)
            for copy in copies_of(piece):
                copy.wait_recv()

    def filter_half(half):
        if half not in filtered:
            filtered.add(half)
            for part in range(ahead_chunks):
                arrive((0, part, half))
            own_copy(half).wait()
            columns(half)

    def finish(part):
        finished.add(part)
        if len(finished) == 1:
            for half in range(halves):
                own_back(half).wait()
        for half in range(halves):
            arrive((1, part, half))
        lax.fori_loop(part * back_chunk, (part + 1) * back_chunk, home, 0)
        twin_copy(part).start()
        shared(part)

    ready = 0
    for place, piece in enumerate(pieces):
        kind, part, half = piece
        if place >= window:
            arrive(pieces[place - window])
        if kind == 0 and part == ready:
            ready += 1
            for copy in direct_copies(part):
                copy.wait_recv()
            for copy in passed_copies(part):
                copy.start()
            if part + 2 < ahead_chunks:
                for copy in direct_copies(part + 2):
                    copy.start()
            for copy in passed_copies(part):
                copy.wait_recv()
            lax.fori_loop(part * ahead_chunk, (part + 1) * ahead_chunk, ahead, 0)
            if ready == ahead_chunks:
                for each in range(halves):
                    own_copy(each).start()
        if kind == 1:
            filter_half(half)
        for copy in copies_of(piece):
            copy.start()
        for each in range(halves):
            if ready == ahead_chunks and all((0, p, each) in arrived for p in range(ahead_chunks)):
                filter_half(each)
        for each in range(back_chunks):
            if each not in finished and all((1, each, h) in arrived for h in range(halves)):
                finish(each)
    for piece in pieces:
        arrive(piece)
        for each in range(back_chunks):
            if each not in finished and all((1, each, h) in arrived for h in range(halves)):
                finish(each)
    for part in range(back_chunks):
        for copy in chip_copies(part):
            copy.wait()
        lax.fori_loop(part * back_chunk, (part + 1) * back_chunk, last, 0)
        twin_copy(part).wait_send()
    for piece in pieces:
        for copy in copies_of(piece):
            copy.wait_send()
    for part in range(ahead_chunks):
        for copy in direct_copies(part) + passed_copies(part):
            copy.wait_send()


def local(orbitals, pivots, pattern):
    orbital = orbitals[0]
    n, bands = lax.axis_size("grid"), lax.axis_size("band")
    planes, length = orbital.shape[0], orbital.shape[2]
    chips = bands // 2
    depth = length // n
    halves = 2 if depth % 16 == 0 else 1
    rows = depth // halves
    ahead_chunks = planes // max(planes // 8, 2)
    back_chunks = planes // max(planes // 8, 2)
    left, right = hartley_tables(length)
    vmem = pl.BlockSpec(memory_space=pltpu.VMEM)
    smem = pl.BlockSpec(memory_space=pltpu.SMEM)
    hbm = pl.BlockSpec(memory_space=pl.ANY)
    slab = jax.ShapeDtypeStruct(orbital.shape, jnp.float32)
    block = planes * rows
    table = (bands, -(-bands // 8) * 8, length)
    dma = pltpu.SemaphoreType.DMA
    localized, exchange_term = pl.pallas_call(
        functools.partial(transform_kernel, n, halves, ahead_chunks, back_chunks, chips, 4, 3),
        out_shape=(slab, slab),
        in_specs=[smem] * 2 + [hbm] * 3,
        out_specs=(vmem, vmem),
        scratch_shapes=[
            pltpu.VMEM((n, halves, 2, block, length), jnp.float32),
            pltpu.VMEM((halves, 2, n * block, length), jnp.float32),
            pltpu.VMEM((halves, 2, n * block, length), jnp.float32),
            pltpu.VMEM((halves, n, 2, block, length), jnp.float32),
            pltpu.VMEM(slab.shape, jnp.float32),
            pltpu.VMEM(slab.shape, jnp.float32),
            pltpu.VMEM(slab.shape, jnp.float32),
            pltpu.VMEM((chips - 1,) + slab.shape, jnp.float32),
            pltpu.VMEM((chips - 1,) + slab.shape, jnp.float32),
            pltpu.VMEM((bands - 1,) + slab.shape, jnp.float32),
            pltpu.VMEM(slab.shape, jnp.float32),
            pltpu.VMEM(left.shape, left.dtype),
            pltpu.VMEM(right.shape, right.dtype),
            pltpu.VMEM((length, length), jnp.float32),
            pltpu.VMEM((2,) + table, jnp.float32),
            pltpu.VMEM((bands - 1,) + table, jnp.float32),
            pltpu.VMEM((n - 1,) + table, jnp.float32),
            pltpu.VMEM((3,) + table[1:], jnp.float32),
            pltpu.SMEM((2, bands), jnp.float32),
            dma((ahead_chunks, halves, n)),
            dma((ahead_chunks, halves, n)),
            dma((back_chunks, halves, n)),
            dma((back_chunks, halves, n)),
            dma((2 * halves,)),
            dma((2, back_chunks)),
            dma((2, back_chunks, chips - 1)),
            dma((2, ahead_chunks, bands - 1)),
            dma((3,)),
            dma((2, bands)),
            dma((2, n)),
        ],
        compiler_params=pltpu.CompilerParams(
            collective_id=0, has_side_effects=True, vmem_limit_bytes=40 * 1024 * 1024
        ),
    )(pivots, pattern, orbital, left, right)
    return (localized[None], exchange_term[None])


def solution(mesh):
    return jax.shard_map(
        local,
        mesh=mesh,
        in_specs=(P("band", "grid", None, None), P(), P()),
        out_specs=(P("band", "grid", None, None), P("band", "grid", None, None)),
        check_vma=False,
    )
```

```python
import functools

import jax
import jax.numpy as jnp
import numpy as np
from jax import lax
from jax.experimental import pallas as pl
from jax.experimental.pallas import tpu as pltpu
from jax.sharding import PartitionSpec as P

MESH = pl.DeviceIdType.MESH


def hartley_table(length):
    across = np.arange(length)
    angles = (across[:, None] * across[None, :] % length) * (2.0 * np.pi / length)
    table = np.cos(angles) + np.sin(angles)
    high = table.astype(jnp.bfloat16)
    low = (table - high.astype(np.float64)).astype(jnp.bfloat16)
    return jnp.asarray(np.stack([high, low]))


def await_bytes(ref, sem):
    pltpu.make_async_copy(ref, ref, sem).wait()


def in_two(values, axis):
    high = values.astype(jnp.bfloat16)
    low = (values - high.astype(jnp.float32)).astype(jnp.bfloat16)
    return jnp.concatenate([high, low], axis=axis)


def along_lanes(values, table):
    length = values.shape[1]
    both = jnp.dot(in_two(values, 1), table, preferred_element_type=jnp.float32)
    return both[:, :length] + both[:, length:]


def along_rows(values, table):
    length = values.shape[0]
    both = jnp.dot(table, in_two(values, 0), preferred_element_type=jnp.float32)
    return both[:length] + both[length:]


def wrapped(indices, length):
    return jnp.where(indices < length // 2, indices, indices - length).astype(jnp.float32)


def transform_kernel(
    n, halves, ahead_chunks, back_chunks, chips, window, lag,
    pivot_hbm, pattern_hbm, orbital_hbm, table_hbm,
    own_hbm, term_hbm,
    send_one, recv_one, send_two, recv_two, second_ref, off_ref, twin_ref, going, coming,
    every_ref, raw_ref, left_ref, right_ref, base_ref, picks, from_band, from_grid, mix_ref, share_ref,
    table_ref, pivot_ref, pattern_ref, own_ref, term_ref,
    sems_one, sems_two, sems_own, sems_twin, sems_chip, sems_in, sems_keep, sems_sent, sems_pick,
):
    bands = every_ref.shape[0] + 1
    planes, length = own_ref.shape[0], own_ref.shape[2]
    me, band_me = lax.axis_index("grid"), lax.axis_index("band")
    chip, core = band_me // 2, lax.rem(band_me, 2)
    partner = chip * 2 + 1 - core
    peers = [lax.rem(chip + step, chips) * 2 + core for step in range(1, chips)]
    sources = [lax.rem(chip + chips - step, chips) * 2 for step in range(1, chips)]
    slots = [low + core for low in sources] + [partner] + [low + 1 - core for low in sources]
    depth = length // n
    rows = depth // halves
    size = planes * rows
    ahead_chunk, back_chunk = planes // ahead_chunks, planes // back_chunks
    barrier = pltpu.get_barrier_semaphore()
    for axis, count, here in (("grid", n, me), ("band", bands, band_me)):
        for step in range(1, count):
            pl.semaphore_signal(
                barrier, inc=1, device_id={axis: lax.rem(here + step, count)}, device_id_type=MESH
            )
    keep = [
        pltpu.make_async_copy(source, target, sems_keep.at[place])
        for place, (source, target) in enumerate(
            ((orbital_hbm, raw_ref), (pivot_hbm, pivot_ref), (table_hbm, table_ref), (pattern_hbm, pattern_ref))
        )
    ]
    for copy in keep:
        copy.start()

    tile = picks.shape[2:]
    sublane = lax.broadcasted_iota(jnp.int32, tile, 0)
    lane = lax.broadcasted_iota(jnp.int32, tile, 1)
    keep[0].wait()
    keep[1].wait()
    slab = planes * length * length
    for column in range(bands):
        cell = pivot_ref[column] - me * slab
        inside = jnp.where((cell >= 0) & (cell < slab), 1, 0)
        cell = jnp.clip(cell, 0, slab - 1)
        row = raw_ref[cell // (length * length), pl.ds(lax.rem(cell // length, length), 1), :]
        mine = (sublane == band_me) & (lane == lax.rem(cell, length)) & (jnp.full(tile, inside) > 0)
        picks[0, column] = jnp.where(mine, jnp.broadcast_to(row, tile), 0.0)
    pl.semaphore_wait(barrier, n + bands - 2)

    def pick_copies(place, axis, count, here, landing):
        return [
            pltpu.make_async_remote_copy(
                src_ref=picks.at[place],
                dst_ref=landing.at[step - 1],
                send_sem=sems_pick.at[place, 0],
                recv_sem=sems_pick.at[place, 1],
                device_id={axis: lax.rem(here + step, count)},
                device_id_type=MESH,
            )
            for step in range(1, count)
        ]

    for copy in pick_copies(0, "band", bands, band_me, from_band):
        copy.start()

    def part_copy(source, part, slot, target, passed):
        place = pl.ds(part * ahead_chunk, ahead_chunk)
        return pltpu.make_async_remote_copy(
            src_ref=source.at[place],
            dst_ref=every_ref.at[slot, place],
            send_sem=sems_sent.at[0],
            recv_sem=sems_in.at[part, passed],
            device_id={"band": target},
            device_id_type=MESH,
        )

    def direct_copies(part):
        return [part_copy(raw_ref, part, slot, target, 0) for slot, target in enumerate(peers + [partner])]

    def passed_copies(part):
        return [
            part_copy(every_ref.at[step - 1], part, chips - 1 + step, partner, 1) for step in range(1, chips)
        ]

    for part in range(min(2, ahead_chunks)):
        for copy in direct_copies(part):
            copy.start()

    await_bytes(from_band, sems_pick.at[0, 1])
    total = picks[0]
    for step in range(bands - 1):
        total = total + from_band[step]
    picks[1] = total
    for copy in pick_copies(1, "grid", n, me, from_grid):
        copy.start()

    waves = [wrapped(lax.broadcasted_iota(jnp.int32, (length, length), axis), length) for axis in range(2)]
    base_ref[...] = waves[0] * waves[0] + waves[1] * waves[1]
    keep[3].wait()
    firsts = [[0.0] * bands for _ in range(2)]
    seconds = [0.0] * bands
    before = 0
    for row in range(bands):
        for column in range(bands):
            if row != column:
                on = jnp.where(pattern_ref[row, column] == 1, 1, 0)
                for place, band in enumerate((band_me, partner)):
                    chosen = jnp.where((on == 1) & (before == band), 1.0, 0.0)
                    firsts[place][row] = firsts[place][row] + chosen
                    if place == 0:
                        seconds[column] = seconds[column] + chosen
                before = before + on
    for place in range(2):
        for band in range(bands):
            share_ref[place, band] = firsts[place][band]

    await_bytes(from_grid, sems_pick.at[1, 1])
    for step in range(n - 1):
        total = total + from_grid[step]
    columns_of = [
        jnp.broadcast_to(jnp.sum(total[column], axis=1, keepdims=True), tile) for column in range(bands)
    ]
    factor = [[None] * bands for _ in range(bands)]
    solved = []
    for row in range(bands):
        for column in range(row + 1):
            value = jnp.sum(columns_of[row] * columns_of[column], axis=0, keepdims=True)
            for step in range(column):
                value = value - factor[row][step] * factor[column][step]
            factor[row][column] = jnp.sqrt(value) if row == column else value / factor[column][column]
        value = columns_of[row]
        for step in range(row):
            value = value - factor[row][step] * solved[step]
        solved.append(value / factor[row][row])
    owns = [jnp.where(band_me == band, 1.0, 0.0) for band in range(bands)]
    for kind, weights in enumerate((owns, firsts[0], seconds)):
        value = weights[0] * solved[0]
        for band in range(1, bands):
            value = value + weights[band] * solved[band]
        mix_ref[kind] = value
    keep[2].wait()
    high, low = table_ref[0], table_ref[1]
    ends = ((0, high), (length, low))
    for start, value in ends:
        for other in (0, length):
            left_ref[pl.ds(start, length), pl.ds(other, length)] = value
            right_ref[pl.ds(other, length), pl.ds(start, length)] = value

    def out_copies(part, half):
        step_size = ahead_chunk * rows
        mine = pl.ds(pl.multiple_of(me * size + part * step_size, step_size), step_size)
        copies = []
        for step in range(1, n):
            target = lax.rem(me + step, n)
            copies.append(
                pltpu.make_async_remote_copy(
                    src_ref=send_one.at[target, half, :, pl.ds(part * step_size, step_size), :],
                    dst_ref=recv_one.at[half, :, mine, :],
                    send_sem=sems_sent.at[1],
                    recv_sem=sems_one.at[part, half],
                    device_id={"grid": target},
                    device_id_type=MESH,
                )
            )
        return copies

    def own_copy(half):
        return pltpu.make_async_copy(
            send_one.at[me, half],
            recv_one.at[half, :, pl.ds(pl.multiple_of(me * size, size), size), :],
            sems_own.at[half],
        )

    def back_copies(part, half):
        step_size = back_chunk * rows
        copies = []
        for step in range(1, n):
            target = lax.rem(me + step, n)
            start = pl.multiple_of(target * size + part * step_size, step_size)
            copies.append(
                pltpu.make_async_remote_copy(
                    src_ref=send_two.at[half, :, pl.ds(start, step_size), :],
                    dst_ref=recv_two.at[half, me, :, pl.ds(part * step_size, step_size), :],
                    send_sem=sems_sent.at[2],
                    recv_sem=sems_two.at[part, half],
                    device_id={"grid": target},
                    device_id_type=MESH,
                )
            )
        return copies

    def own_back(half):
        return pltpu.make_async_copy(
            send_two.at[half, :, pl.ds(pl.multiple_of(me * size, size), size), :],
            recv_two.at[half, me],
            sems_own.at[halves + half],
        )

    def ahead(plane, carry):
        values = [raw_ref[plane]] + [every_ref[slot, plane] for slot in range(bands - 1)]
        parts = []
        for kind in range(3):
            value = mix_ref[kind, pl.ds(band_me, 1), :] * values[0]
            for slot in range(bands - 1):
                value = value + mix_ref[kind, pl.ds(slots[slot], 1), :] * values[slot + 1]
            parts.append(value)
        own, first, second = parts
        own_ref[plane] = own
        second_ref[plane] = second
        both = jnp.concatenate([own * own, first * second], axis=0)
        spectrum = along_lanes(both, right_ref[...])
        result = along_rows(
            jnp.concatenate([spectrum[:length], spectrum[length:]], axis=1), left_ref[...]
        )
        for target in range(n):
            for half in range(halves):
                for part in range(2):
                    low = target * depth + half * rows
                    send_one[target, half, part, pl.ds(plane * rows, rows), :] = (
                        result[low : low + rows, part * length : (part + 1) * length]
                    )
        return carry

    def columns(half):
        def step(row, carry):
            place = pl.ds(row, length, stride=rows)
            both = jnp.concatenate(
                [recv_one[half, 0, place, :], recv_one[half, 1, place, :]], axis=1
            )
            wave = wrapped(me * depth + half * rows + row, length)
            squared = base_ref[...] + wave * wave
            scaling = float(length) ** 1.5
            weights = jnp.where(
                squared > 0, 0.25 / (scaling * jnp.maximum(squared, 1.0)), 0.0
            )
            spectrum = along_rows(both, left_ref[...])
            spectrum = spectrum * jnp.concatenate([weights, weights], axis=1)
            result = along_rows(spectrum, left_ref[...])
            send_two[half, 0, place, :] = result[:, :length]
            send_two[half, 1, place, :] = result[:, length:]
            return carry

        lax.fori_loop(0, rows, step, 0)
        own_back(half).start()

    def twin_copy(part):
        place = pl.ds(part * back_chunk, back_chunk)
        return pltpu.make_async_remote_copy(
            src_ref=off_ref.at[place],
            dst_ref=twin_ref.at[place],
            send_sem=sems_sent.at[3],
            recv_sem=sems_twin.at[part],
            device_id={"band": partner},
            device_id_type=MESH,
        )

    def chip_copies(part):
        place = pl.ds(part * back_chunk, back_chunk)
        return [
            pltpu.make_async_remote_copy(
                src_ref=going.at[step, place],
                dst_ref=coming.at[step, place],
                send_sem=sems_sent.at[4],
                recv_sem=sems_chip.at[part],
                device_id={"band": peer},
                device_id_type=MESH,
            )
            for step, peer in enumerate(peers)
        ]

    def shared(part):
        await_bytes(twin_ref.at[pl.ds(part * back_chunk, back_chunk)], sems_twin.at[part])

        def one(plane, carry):
            mine, other = off_ref[plane], twin_ref[plane]
            for step, peer in enumerate(peers):
                going[step, plane] = share_ref[0, peer] * mine + share_ref[1, peer] * other
            term_ref[plane] = (
                term_ref[plane] + share_ref[0, band_me] * mine + share_ref[1, band_me] * other
            )
            return carry

        lax.fori_loop(part * back_chunk, (part + 1) * back_chunk, one, 0)
        for copy in chip_copies(part):
            copy.start()

    def home(plane, carry):
        place = pl.ds(plane * rows, rows)
        both = jnp.concatenate(
            [
                jnp.concatenate(
                    [recv_two[half, source, part, place, :] for source in range(n) for half in range(halves)],
                    axis=0,
                )
                for part in range(2)
            ],
            axis=1,
        )
        result = along_rows(both, left_ref[...])
        potential = along_lanes(
            jnp.concatenate([result[:, :length], result[:, length:]], axis=0), right_ref[...]
        )
        term_ref[plane] = potential[:length] * own_ref[plane]
        off_ref[plane] = potential[length:] * second_ref[plane]
        return carry

    def last(plane, carry):
        total = term_ref[plane]
        for step in range(chips - 1):
            total = total + coming[step, plane]
        term_ref[plane] = total
        return carry

    def copies_of(piece):
        kind, part, half = piece
        return back_copies(part, half) if kind else out_copies(part, half)

    forward, late = [], []
    for part in range(ahead_chunks):
        forward.append((0, part, 0))
        late.extend((0, part, half) for half in range(1, halves))
        if part % 2 == 1 and part < ahead_chunks - 1 and late:
            forward.append(late.pop(0))
    forward = forward + late
    backward = []
    for place in range(back_chunks + lag * (halves - 1)):
        for half in range(halves):
            if 0 <= place - lag * half < back_chunks:
                backward.append((1, place - lag * half, half))
    pieces = forward + backward
    arrived, filtered, finished = set(), set(), set()

    def arrive(piece):
        if piece not in arrived:
            arrived.add(piece)
            kind, part, half = piece
            if kind:
                taken = pl.ds(0, back_chunk * rows)
                await_bytes(recv_two.at[half, pl.ds(0, n - 1), :, taken, :], sems_two.at[part, half])
            else:
                taken = pl.ds(0, (n - 1) * ahead_chunk * rows)
                await_bytes(recv_one.at[half, :, taken, :], sems_one.at[part, half])

    def filter_half(half):
        if half not in filtered:
            filtered.add(half)
            for part in range(ahead_chunks):
                arrive((0, part, half))
            own_copy(half).wait()
            columns(half)

    def finish(part):
        finished.add(part)
        if len(finished) == 1:
            for half in range(halves):
                own_back(half).wait()
        for half in range(halves):
            arrive((1, part, half))
        lax.fori_loop(part * back_chunk, (part + 1) * back_chunk, home, 0)
        twin_copy(part).start()
        shared(part)

    ready = 0
    for index, piece in enumerate(pieces):
        kind, part, half = piece
        if index >= window:
            arrive(pieces[index - window])
        if kind == 0 and part == ready:
            ready += 1
            place = pl.ds(part * ahead_chunk, ahead_chunk)
            await_bytes(every_ref.at[pl.ds(0, chips), place], sems_in.at[part, 0])
            for copy in passed_copies(part):
                copy.start()
            if part + 2 < ahead_chunks:
                for copy in direct_copies(part + 2):
                    copy.start()
            await_bytes(every_ref.at[pl.ds(chips, chips - 1), place], sems_in.at[part, 1])
            lax.fori_loop(part * ahead_chunk, (part + 1) * ahead_chunk, ahead, 0)
            if ready == ahead_chunks:
                for each in range(halves):
                    own_copy(each).start()
        if kind == 1:
            filter_half(half)
        for copy in copies_of(piece):
            copy.start()
        for each in range(halves):
            if ready == ahead_chunks and all((0, p, each) in arrived for p in range(ahead_chunks)):
                filter_half(each)
        for each in range(back_chunks):
            if each not in finished and all((1, each, h) in arrived for h in range(halves)):
                finish(each)
    for piece in pieces:
        arrive(piece)
        for each in range(back_chunks):
            if each not in finished and all((1, each, h) in arrived for h in range(halves)):
                finish(each)
    result = [pltpu.make_async_copy(own_ref, own_hbm, sems_keep.at[4])]
    result[0].start()
    for part in range(back_chunks):
        place = pl.ds(part * back_chunk, back_chunk)
        await_bytes(coming.at[:, place], sems_chip.at[part])
        lax.fori_loop(part * back_chunk, (part + 1) * back_chunk, last, 0)
    await_bytes(from_band, sems_pick.at[0, 0])
    await_bytes(from_grid, sems_pick.at[1, 0])
    await_bytes(every_ref, sems_sent.at[0])
    await_bytes(send_one.at[pl.ds(0, n - 1)], sems_sent.at[1])
    await_bytes(send_two.at[:, :, pl.ds(0, (n - 1) * size), :], sems_sent.at[2])
    await_bytes(off_ref, sems_sent.at[3])
    await_bytes(going, sems_sent.at[4])
    result.append(pltpu.make_async_copy(term_ref, term_hbm, sems_keep.at[5]))
    result[1].start()
    for copy in result:
        copy.wait()


def local(orbitals, pivots, pattern):
    orbital = orbitals[0]
    n, bands = lax.axis_size("grid"), lax.axis_size("band")
    planes, length = orbital.shape[0], orbital.shape[2]
    chips = bands // 2
    depth = length // n
    halves = 2 if depth % 16 == 0 else 1
    rows = depth // halves
    ahead_chunks = planes // max(planes // 8, 2)
    back_chunks = planes // max(planes // 8, 2)
    table = hartley_table(length)
    hbm = pl.BlockSpec(memory_space=pl.ANY)
    slab = jax.ShapeDtypeStruct(orbital.shape, jnp.float32)
    block = planes * rows
    shape = (bands, -(-bands // 8) * 8, length)
    dma = pltpu.SemaphoreType.DMA
    localized, exchange_term = pl.pallas_call(
        functools.partial(transform_kernel, n, halves, ahead_chunks, back_chunks, chips, 4, 3),
        out_shape=(slab, slab),
        in_specs=[hbm] * 4,
        out_specs=(hbm, hbm),
        scratch_shapes=[
            pltpu.VMEM((n, halves, 2, block, length), jnp.float32),
            pltpu.VMEM((halves, 2, n * block, length), jnp.float32),
            pltpu.VMEM((halves, 2, n * block, length), jnp.float32),
            pltpu.VMEM((halves, n, 2, block, length), jnp.float32),
            pltpu.VMEM(slab.shape, jnp.float32),
            pltpu.VMEM(slab.shape, jnp.float32),
            pltpu.VMEM(slab.shape, jnp.float32),
            pltpu.VMEM((chips - 1,) + slab.shape, jnp.float32),
            pltpu.VMEM((chips - 1,) + slab.shape, jnp.float32),
            pltpu.VMEM((bands - 1,) + slab.shape, jnp.float32),
            pltpu.VMEM(slab.shape, jnp.float32),
            pltpu.VMEM((2 * length, 2 * length), table.dtype),
            pltpu.VMEM((2 * length, 2 * length), table.dtype),
            pltpu.VMEM((length, length), jnp.float32),
            pltpu.VMEM((2,) + shape, jnp.float32),
            pltpu.VMEM((bands - 1,) + shape, jnp.float32),
            pltpu.VMEM((n - 1,) + shape, jnp.float32),
            pltpu.VMEM((3,) + shape[1:], jnp.float32),
            pltpu.SMEM((2, bands), jnp.float32),
            pltpu.VMEM(table.shape, table.dtype),
            pltpu.SMEM(pivots.shape, jnp.int32),
            pltpu.SMEM(pattern.shape, jnp.int32),
            pltpu.VMEM(slab.shape, jnp.float32),
            pltpu.VMEM(slab.shape, jnp.float32),
            dma((ahead_chunks, halves)),
            dma((back_chunks, halves)),
            dma((2 * halves,)),
            dma((back_chunks,)),
            dma((back_chunks,)),
            dma((ahead_chunks, 2)),
            dma((6,)),
            dma((5,)),
            dma((2, 2)),
        ],
        compiler_params=pltpu.CompilerParams(
            collective_id=0, has_side_effects=True, vmem_limit_bytes=62 * 1024 * 1024
        ),
    )(pivots, pattern, orbital, table)
    return (localized[None], exchange_term[None])


def solution(mesh):
    return jax.shard_map(
        local,
        mesh=mesh,
        in_specs=(P("band", "grid", None, None), P(), P()),
        out_specs=(P("band", "grid", None, None), P("band", "grid", None, None)),
        check_vma=False,
    )
```

```python
import functools

import jax
import jax.numpy as jnp
import numpy as np
from jax import lax
from jax.experimental import pallas as pl
from jax.experimental.pallas import tpu as pltpu
from jax.sharding import PartitionSpec as P

MESH = pl.DeviceIdType.MESH


def hartley_table(length):
    across = np.arange(length)
    angles = (across[:, None] * across[None, :] % length) * (2.0 * np.pi / length)
    table = np.cos(angles) + np.sin(angles)
    high = table.astype(jnp.bfloat16)
    low = (table - high.astype(np.float64)).astype(jnp.bfloat16)
    return jnp.asarray(np.stack([high, low]))


def await_bytes(ref, sem):
    pltpu.make_async_copy(ref, ref, sem).wait()


def in_two(values, axis):
    high = values.astype(jnp.bfloat16)
    low = (values - high.astype(jnp.float32)).astype(jnp.bfloat16)
    return jnp.concatenate([high, low], axis=axis)


def along_lanes(values, table):
    length = values.shape[1]
    both = jnp.dot(in_two(values, 1), table, preferred_element_type=jnp.float32)
    return both[:, :length] + both[:, length:]


def along_rows(values, table):
    length = values.shape[0]
    both = jnp.dot(table, in_two(values, 0), preferred_element_type=jnp.float32)
    return both[:length] + both[length:]


def wrapped(indices, length):
    return jnp.where(indices < length // 2, indices, indices - length).astype(jnp.float32)


def transform_kernel(
    n, halves, ahead_sizes, back_sizes, chips, window, lag,
    pivot_hbm, pattern_hbm, orbital_hbm, table_hbm,
    own_hbm, term_hbm,
    send_one, recv_one, send_two, recv_two, second_ref, off_ref, twin_ref, going, coming,
    every_ref, raw_ref, left_ref, right_ref, base_ref, picks, told, mix_ref, share_ref,
    table_ref, pivot_ref, pattern_ref, own_ref, term_ref,
    sems_one, sems_two, sems_own, sems_twin, sems_chip, sems_in, sems_keep, sems_sent, sems_pick,
):
    bands = every_ref.shape[0] + 1
    planes, length = own_ref.shape[0], own_ref.shape[2]
    me, band_me = lax.axis_index("grid"), lax.axis_index("band")
    chip, core = band_me // 2, lax.rem(band_me, 2)
    partner = chip * 2 + 1 - core
    peers = [lax.rem(chip + step, chips) * 2 + core for step in range(1, chips)]
    sources = [lax.rem(chip + chips - step, chips) * 2 for step in range(1, chips)]
    slots = [low + core for low in sources] + [partner] + [low + 1 - core for low in sources]
    depth = length // n
    rows = depth // halves
    size = planes * rows
    ahead_chunks, back_chunks = len(ahead_sizes), len(back_sizes)
    ahead_starts = [sum(ahead_sizes[:part]) for part in range(ahead_chunks + 1)]
    back_starts = [sum(back_sizes[:part]) for part in range(back_chunks + 1)]
    barrier = pltpu.get_barrier_semaphore()

    def other(step):
        return {
            "band": lax.rem(band_me + step // n, bands),
            "grid": lax.rem(me + lax.rem(step, n), n),
        }

    def greet(step, carry):
        pl.semaphore_signal(barrier, inc=1, device_id=other(step), device_id_type=MESH)
        return carry

    lax.fori_loop(1, n * bands, greet, 0)
    keep = [
        pltpu.make_async_copy(source, target, sems_keep.at[place])
        for place, (source, target) in enumerate(
            ((orbital_hbm, raw_ref), (pivot_hbm, pivot_ref), (table_hbm, table_ref), (pattern_hbm, pattern_ref))
        )
    ]
    for copy in keep:
        copy.start()

    tile = picks.shape
    sublane = lax.broadcasted_iota(jnp.int32, tile, 0)
    lane = lax.broadcasted_iota(jnp.int32, tile, 1)
    keep[0].wait()
    keep[1].wait()
    slab = planes * length * length
    sampled = jnp.zeros((1, length), jnp.float32)
    for column in range(bands):
        cell = pivot_ref[column] - me * slab
        inside = jnp.where((cell >= 0) & (cell < slab), 1, 0)
        cell = jnp.clip(cell, 0, slab - 1)
        row = raw_ref[cell // (length * length), pl.ds(lax.rem(cell // length, length), 1), :]
        chosen = (lane[:1] == lax.rem(cell, length)) & (jnp.full((1, length), inside) > 0)
        value = jnp.sum(jnp.where(chosen, row, 0.0), axis=1, keepdims=True)
        sampled = sampled + jnp.where(lane[:1] == column, value, 0.0)
    picks[...] = jnp.where(sublane == band_me, jnp.broadcast_to(sampled, tile), 0.0)
    pl.semaphore_wait(barrier, n * bands - 1)

    def tell(step, carry):
        pltpu.make_async_remote_copy(
            src_ref=picks,
            dst_ref=told.at[step - 1],
            send_sem=sems_pick.at[0],
            recv_sem=sems_pick.at[1],
            device_id=other(step),
            device_id_type=MESH,
        ).start()
        return carry

    lax.fori_loop(1, n * bands, tell, 0)

    def part_copy(source, part, slot, target, passed):
        place = pl.ds(ahead_starts[part], ahead_sizes[part])
        return pltpu.make_async_remote_copy(
            src_ref=source.at[place],
            dst_ref=every_ref.at[slot, place],
            send_sem=sems_sent.at[0],
            recv_sem=sems_in.at[part, passed],
            device_id={"band": target},
            device_id_type=MESH,
        )

    def direct_copies(part):
        return [part_copy(raw_ref, part, slot, target, 0) for slot, target in enumerate(peers + [partner])]

    def passed_copies(part):
        return [
            part_copy(every_ref.at[step - 1], part, chips - 1 + step, partner, 1) for step in range(1, chips)
        ]

    for part in range(min(2, ahead_chunks)):
        for copy in direct_copies(part):
            copy.start()

    waves = [wrapped(lax.broadcasted_iota(jnp.int32, (length, length), axis), length) for axis in range(2)]
    base_ref[...] = waves[0] * waves[0] + waves[1] * waves[1]
    keep[3].wait()
    firsts = [[0.0] * bands for _ in range(2)]
    seconds = [0.0] * bands
    before = 0
    for row in range(bands):
        for column in range(bands):
            if row != column:
                on = jnp.where(pattern_ref[row, column] == 1, 1, 0)
                for place, band in enumerate((band_me, partner)):
                    chosen = jnp.where((on == 1) & (before == band), 1.0, 0.0)
                    firsts[place][row] = firsts[place][row] + chosen
                    if place == 0:
                        seconds[column] = seconds[column] + chosen
                before = before + on
    for place in range(2):
        for band in range(bands):
            share_ref[place, band] = firsts[place][band]

    await_bytes(told, sems_pick.at[1])
    total = picks[...] + jnp.sum(told[...], axis=0)
    columns_of = [
        jnp.broadcast_to(
            jnp.sum(jnp.where(lane == column, total, 0.0), axis=1, keepdims=True), tile
        )
        for column in range(bands)
    ]
    factor = [[None] * bands for _ in range(bands)]
    solved = []
    for row in range(bands):
        for column in range(row + 1):
            value = jnp.sum(columns_of[row] * columns_of[column], axis=0, keepdims=True)
            for step in range(column):
                value = value - factor[row][step] * factor[column][step]
            factor[row][column] = jnp.sqrt(value) if row == column else value / factor[column][column]
        value = columns_of[row]
        for step in range(row):
            value = value - factor[row][step] * solved[step]
        solved.append(value / factor[row][row])
    owns = [jnp.where(band_me == band, 1.0, 0.0) for band in range(bands)]
    for kind, weights in enumerate((owns, firsts[0], seconds)):
        value = weights[0] * solved[0]
        for band in range(1, bands):
            value = value + weights[band] * solved[band]
        mix_ref[kind] = value
    keep[2].wait()
    high, low = table_ref[0], table_ref[1]
    ends = ((0, high), (length, low))
    for start, value in ends:
        for other in (0, length):
            left_ref[pl.ds(start, length), pl.ds(other, length)] = value
            right_ref[pl.ds(other, length), pl.ds(start, length)] = value

    def out_copies(part, half):
        start, step_size = ahead_starts[part] * rows, ahead_sizes[part] * rows
        mine = pl.ds(pl.multiple_of(me * size + start, 8), step_size)
        copies = []
        for step in range(1, n):
            target = lax.rem(me + step, n)
            copies.append(
                pltpu.make_async_remote_copy(
                    src_ref=send_one.at[target, half, :, pl.ds(start, step_size), :],
                    dst_ref=recv_one.at[half, :, mine, :],
                    send_sem=sems_sent.at[1],
                    recv_sem=sems_one.at[part, half],
                    device_id={"grid": target},
                    device_id_type=MESH,
                )
            )
        return copies

    def own_copy(half):
        return pltpu.make_async_copy(
            send_one.at[me, half],
            recv_one.at[half, :, pl.ds(pl.multiple_of(me * size, size), size), :],
            sems_own.at[half],
        )

    def back_copies(part, half):
        start, step_size = back_starts[part] * rows, back_sizes[part] * rows
        copies = []
        for step in range(1, n):
            target = lax.rem(me + step, n)
            place = pl.ds(pl.multiple_of(target * size + start, 8), step_size)
            copies.append(
                pltpu.make_async_remote_copy(
                    src_ref=send_two.at[half, :, place, :],
                    dst_ref=recv_two.at[half, me, :, pl.ds(start, step_size), :],
                    send_sem=sems_sent.at[2],
                    recv_sem=sems_two.at[part, half],
                    device_id={"grid": target},
                    device_id_type=MESH,
                )
            )
        return copies

    def own_back(half):
        return pltpu.make_async_copy(
            send_two.at[half, :, pl.ds(pl.multiple_of(me * size, size), size), :],
            recv_two.at[half, me],
            sems_own.at[halves + half],
        )

    def ahead(plane, carry):
        values = [raw_ref[plane]] + [every_ref[slot, plane] for slot in range(bands - 1)]
        parts = []
        for kind in range(3):
            value = mix_ref[kind, pl.ds(band_me, 1), :] * values[0]
            for slot in range(bands - 1):
                value = value + mix_ref[kind, pl.ds(slots[slot], 1), :] * values[slot + 1]
            parts.append(value)
        own, first, second = parts
        own_ref[plane] = own
        second_ref[plane] = second
        both = jnp.concatenate([own * own, first * second], axis=0)
        spectrum = along_lanes(both, right_ref[...])
        result = along_rows(
            jnp.concatenate([spectrum[:length], spectrum[length:]], axis=1), left_ref[...]
        )
        for target in range(n):
            for half in range(halves):
                for part in range(2):
                    low = target * depth + half * rows
                    send_one[target, half, part, pl.ds(plane * rows, rows), :] = (
                        result[low : low + rows, part * length : (part + 1) * length]
                    )
        return carry

    def columns(half):
        def step(row, carry):
            place = pl.ds(row, length, stride=rows)
            both = jnp.concatenate(
                [recv_one[half, 0, place, :], recv_one[half, 1, place, :]], axis=1
            )
            wave = wrapped(me * depth + half * rows + row, length)
            squared = base_ref[...] + wave * wave
            scaling = float(length) ** 1.5
            weights = jnp.where(
                squared > 0, 0.25 / (scaling * jnp.maximum(squared, 1.0)), 0.0
            )
            spectrum = along_rows(both, left_ref[...])
            spectrum = spectrum * jnp.concatenate([weights, weights], axis=1)
            result = along_rows(spectrum, left_ref[...])
            send_two[half, 0, place, :] = result[:, :length]
            send_two[half, 1, place, :] = result[:, length:]
            return carry

        lax.fori_loop(0, rows, step, 0)
        own_back(half).start()

    def twin_copy(part):
        place = pl.ds(back_starts[part], back_sizes[part])
        return pltpu.make_async_remote_copy(
            src_ref=off_ref.at[place],
            dst_ref=twin_ref.at[place],
            send_sem=sems_sent.at[3],
            recv_sem=sems_twin.at[part],
            device_id={"band": partner},
            device_id_type=MESH,
        )

    def chip_copies(part):
        place = pl.ds(back_starts[part], back_sizes[part])
        return [
            pltpu.make_async_remote_copy(
                src_ref=going.at[step, place],
                dst_ref=coming.at[step, place],
                send_sem=sems_sent.at[4],
                recv_sem=sems_chip.at[part],
                device_id={"band": peer},
                device_id_type=MESH,
            )
            for step, peer in enumerate(peers)
        ]

    def shared(part):
        await_bytes(twin_ref.at[pl.ds(back_starts[part], back_sizes[part])], sems_twin.at[part])

        def one(plane, carry):
            mine, other = off_ref[plane], twin_ref[plane]
            for step, peer in enumerate(peers):
                going[step, plane] = share_ref[0, peer] * mine + share_ref[1, peer] * other
            term_ref[plane] = (
                term_ref[plane] + share_ref[0, band_me] * mine + share_ref[1, band_me] * other
            )
            return carry

        lax.fori_loop(back_starts[part], back_starts[part + 1], one, 0)
        for copy in chip_copies(part):
            copy.start()

    def home(plane, carry):
        place = pl.ds(plane * rows, rows)
        both = jnp.concatenate(
            [
                jnp.concatenate(
                    [recv_two[half, source, part, place, :] for source in range(n) for half in range(halves)],
                    axis=0,
                )
                for part in range(2)
            ],
            axis=1,
        )
        result = along_rows(both, left_ref[...])
        potential = along_lanes(
            jnp.concatenate([result[:, :length], result[:, length:]], axis=0), right_ref[...]
        )
        term_ref[plane] = potential[:length] * own_ref[plane]
        off_ref[plane] = potential[length:] * second_ref[plane]
        return carry

    def last(plane, carry):
        total = term_ref[plane]
        for step in range(chips - 1):
            total = total + coming[step, plane]
        term_ref[plane] = total
        return carry

    def copies_of(piece):
        kind, part, half = piece
        return back_copies(part, half) if kind else out_copies(part, half)

    forward, late = [], []
    for part in range(ahead_chunks):
        forward.append((0, part, 0))
        late.extend((0, part, half) for half in range(1, halves))
        if part % 2 == 1 and part < ahead_chunks - 1 and late:
            forward.append(late.pop(0))
    forward = forward + late
    backward = []
    for place in range(back_chunks + lag * (halves - 1)):
        for half in range(halves):
            if 0 <= place - lag * half < back_chunks:
                backward.append((1, place - lag * half, half))
    pieces = forward + backward
    arrived, filtered, finished = set(), set(), set()

    def arrive(piece):
        if piece not in arrived:
            arrived.add(piece)
            kind, part, half = piece
            if kind:
                taken = pl.ds(0, back_sizes[part] * rows)
                await_bytes(recv_two.at[half, pl.ds(0, n - 1), :, taken, :], sems_two.at[part, half])
            else:
                taken = pl.ds(0, (n - 1) * ahead_sizes[part] * rows)
                await_bytes(recv_one.at[half, :, taken, :], sems_one.at[part, half])

    def filter_half(half):
        if half not in filtered:
            filtered.add(half)
            for part in range(ahead_chunks):
                arrive((0, part, half))
            own_copy(half).wait()
            columns(half)

    def finish(part):
        finished.add(part)
        if len(finished) == 1:
            for half in range(halves):
                own_back(half).wait()
        for half in range(halves):
            arrive((1, part, half))
        lax.fori_loop(back_starts[part], back_starts[part + 1], home, 0)
        twin_copy(part).start()
        shared(part)

    ready = 0
    for index, piece in enumerate(pieces):
        kind, part, half = piece
        if index >= window:
            arrive(pieces[index - window])
        if kind == 0 and part == ready:
            ready += 1
            place = pl.ds(ahead_starts[part], ahead_sizes[part])
            await_bytes(every_ref.at[pl.ds(0, chips), place], sems_in.at[part, 0])
            for copy in passed_copies(part):
                copy.start()
            if part + 2 < ahead_chunks:
                for copy in direct_copies(part + 2):
                    copy.start()
            await_bytes(every_ref.at[pl.ds(chips, chips - 1), place], sems_in.at[part, 1])
            lax.fori_loop(ahead_starts[part], ahead_starts[part + 1], ahead, 0)
            if ready == ahead_chunks:
                for each in range(halves):
                    own_copy(each).start()
        if kind == 1:
            filter_half(half)
        for copy in copies_of(piece):
            copy.start()
        for each in range(halves):
            if ready == ahead_chunks and all((0, p, each) in arrived for p in range(ahead_chunks)):
                filter_half(each)
        for each in range(back_chunks):
            if each not in finished and all((1, each, h) in arrived for h in range(halves)):
                finish(each)
    for piece in pieces:
        arrive(piece)
        for each in range(back_chunks):
            if each not in finished and all((1, each, h) in arrived for h in range(halves)):
                finish(each)
    result = [pltpu.make_async_copy(own_ref, own_hbm, sems_keep.at[4])]
    result[0].start()
    for part in range(back_chunks):
        place = pl.ds(back_starts[part], back_sizes[part])
        await_bytes(coming.at[:, place], sems_chip.at[part])
        lax.fori_loop(back_starts[part], back_starts[part + 1], last, 0)
    await_bytes(told, sems_pick.at[0])
    await_bytes(every_ref, sems_sent.at[0])
    await_bytes(send_one.at[pl.ds(0, n - 1)], sems_sent.at[1])
    await_bytes(send_two.at[:, :, pl.ds(0, (n - 1) * size), :], sems_sent.at[2])
    await_bytes(off_ref, sems_sent.at[3])
    await_bytes(going, sems_sent.at[4])
    result.append(pltpu.make_async_copy(term_ref, term_hbm, sems_keep.at[5]))
    result[1].start()
    for copy in result:
        copy.wait()


def place_kernel(first_ref, second_ref, out_first, out_second, held, sems):
    jobs = ((first_ref, out_first), (second_ref, out_second))
    loads = [
        pltpu.make_async_copy(source, held.at[place], sems.at[0, place])
        for place, (source, _) in enumerate(jobs)
    ]
    stores = [
        pltpu.make_async_copy(held.at[place], target, sems.at[1, place])
        for place, (_, target) in enumerate(jobs)
    ]
    for load in loads:
        load.start()
    for load, store in zip(loads, stores):
        load.wait()
        store.start()
    for store in stores:
        store.wait()


def placed(first, second):
    hbm = pl.BlockSpec(memory_space=pl.ANY)
    return pl.pallas_call(
        place_kernel,
        out_shape=(jax.ShapeDtypeStruct(first.shape, jnp.float32),) * 2,
        in_specs=[hbm] * 2,
        out_specs=(hbm, hbm),
        scratch_shapes=[
            pltpu.VMEM((2,) + first.shape, jnp.float32),
            pltpu.SemaphoreType.DMA((2, 2)),
        ],
        compiler_params=pltpu.CompilerParams(vmem_limit_bytes=62 * 1024 * 1024),
    )(first, second)


def local(orbitals, pivots, pattern):
    orbital = orbitals[0]
    n, bands = lax.axis_size("grid"), lax.axis_size("band")
    planes, length = orbital.shape[0], orbital.shape[2]
    chips = bands // 2
    depth = length // n
    halves = 2 if depth % 16 == 0 else 1
    rows = depth // halves
    unit = planes // 16
    small = (2,) * (planes // 2)
    ahead_sizes = tuple(unit * size for size in (1, 1, 2, 2, 2, 2, 2, 2, 2)) if unit else small
    back_sizes = tuple(unit * size for size in (2, 2, 2, 2, 2, 2, 2, 1, 1)) if unit else small
    ahead_chunks, back_chunks = len(ahead_sizes), len(back_sizes)
    table = hartley_table(length)
    hbm = pl.BlockSpec(memory_space=pl.ANY)
    slab = jax.ShapeDtypeStruct(orbital.shape, jnp.float32)
    block = planes * rows
    tile = (-(-bands // 8) * 8, length)
    dma = pltpu.SemaphoreType.DMA
    localized, exchange_term = pl.pallas_call(
        functools.partial(transform_kernel, n, halves, ahead_sizes, back_sizes, chips, 4, 3),
        out_shape=(slab, slab),
        in_specs=[hbm] * 4,
        out_specs=(hbm, hbm),
        scratch_shapes=[
            pltpu.VMEM((n, halves, 2, block, length), jnp.float32),
            pltpu.VMEM((halves, 2, n * block, length), jnp.float32),
            pltpu.VMEM((halves, 2, n * block, length), jnp.float32),
            pltpu.VMEM((halves, n, 2, block, length), jnp.float32),
            pltpu.VMEM(slab.shape, jnp.float32),
            pltpu.VMEM(slab.shape, jnp.float32),
            pltpu.VMEM(slab.shape, jnp.float32),
            pltpu.VMEM((chips - 1,) + slab.shape, jnp.float32),
            pltpu.VMEM((chips - 1,) + slab.shape, jnp.float32),
            pltpu.VMEM((bands - 1,) + slab.shape, jnp.float32),
            pltpu.VMEM(slab.shape, jnp.float32),
            pltpu.VMEM((2 * length, 2 * length), table.dtype),
            pltpu.VMEM((2 * length, 2 * length), table.dtype),
            pltpu.VMEM((length, length), jnp.float32),
            pltpu.VMEM(tile, jnp.float32),
            pltpu.VMEM((n * bands - 1,) + tile, jnp.float32),
            pltpu.VMEM((3,) + tile, jnp.float32),
            pltpu.SMEM((2, bands), jnp.float32),
            pltpu.VMEM(table.shape, table.dtype),
            pltpu.SMEM(pivots.shape, jnp.int32),
            pltpu.SMEM(pattern.shape, jnp.int32),
            pltpu.VMEM(slab.shape, jnp.float32),
            pltpu.VMEM(slab.shape, jnp.float32),
            dma((ahead_chunks, halves)),
            dma((back_chunks, halves)),
            dma((2 * halves,)),
            dma((back_chunks,)),
            dma((back_chunks,)),
            dma((ahead_chunks, 2)),
            dma((6,)),
            dma((5,)),
            dma((2,)),
        ],
        compiler_params=pltpu.CompilerParams(
            collective_id=0, has_side_effects=True, vmem_limit_bytes=62 * 1024 * 1024
        ),
    )(pivots, pattern, orbital, table)
    localized, exchange_term = placed(localized, exchange_term)
    return (localized[None], exchange_term[None])


def solution(mesh):
    return jax.shard_map(
        local,
        mesh=mesh,
        in_specs=(P("band", "grid", None, None), P(), P()),
        out_specs=(P("band", "grid", None, None), P("band", "grid", None, None)),
        check_vma=False,
    )
```

```python
import functools

import jax
import jax.numpy as jnp
import numpy as np
from jax import lax
from jax.experimental import pallas as pl
from jax.experimental.pallas import tpu as pltpu
from jax.sharding import PartitionSpec as P

MESH = pl.DeviceIdType.MESH


def hartley_table(length):
    across = np.arange(length)
    angles = (across[:, None] * across[None, :] % length) * (2.0 * np.pi / length)
    table = np.cos(angles) + np.sin(angles)
    high = table.astype(jnp.bfloat16)
    low = (table - high.astype(np.float64)).astype(jnp.bfloat16)
    return jnp.asarray(np.stack([high, low]))


def await_bytes(ref, sem):
    pltpu.make_async_copy(ref, ref, sem).wait()


def in_two(values, axis):
    high = values.astype(jnp.bfloat16)
    low = (values - high.astype(jnp.float32)).astype(jnp.bfloat16)
    return jnp.concatenate([high, low], axis=axis)


def along_lanes(values, table):
    length = values.shape[1]
    both = jnp.dot(in_two(values, 1), table, preferred_element_type=jnp.float32)
    return both[:, :length] + both[:, length:]


def along_rows(values, table):
    length = values.shape[0]
    both = jnp.dot(table, in_two(values, 0), preferred_element_type=jnp.float32)
    return both[:length] + both[length:]


def wrapped(indices, length):
    return jnp.where(indices < length // 2, indices, indices - length).astype(jnp.float32)


def transform_kernel(
    n, halves, ahead_sizes, back_sizes, chips, window, lag,
    pivot_hbm, pattern_hbm, orbital_hbm, table_hbm,
    own_ref, term_ref,
    send_one, recv_one, send_two, recv_two, second_ref, off_ref, twin_ref, going, coming,
    every_ref, raw_ref, left_ref, right_ref, base_ref, picks, told, mix_ref, share_ref,
    table_ref, pivot_ref, pattern_ref,
    sems_one, sems_two, sems_own, sems_twin, sems_chip, sems_in, sems_keep, sems_sent, sems_pick,
):
    bands = every_ref.shape[0] + 1
    planes, length = own_ref.shape[0], own_ref.shape[2]
    me, band_me = lax.axis_index("grid"), lax.axis_index("band")
    chip, core = band_me // 2, lax.rem(band_me, 2)
    partner = chip * 2 + 1 - core
    peers = [lax.rem(chip + step, chips) * 2 + core for step in range(1, chips)]
    sources = [lax.rem(chip + chips - step, chips) * 2 for step in range(1, chips)]
    slots = [low + core for low in sources] + [partner] + [low + 1 - core for low in sources]
    depth = length // n
    rows = depth // halves
    size = planes * rows
    ahead_chunks, back_chunks = len(ahead_sizes), len(back_sizes)
    ahead_starts = [sum(ahead_sizes[:part]) for part in range(ahead_chunks + 1)]
    back_starts = [sum(back_sizes[:part]) for part in range(back_chunks + 1)]
    barrier = pltpu.get_barrier_semaphore()

    def other(step):
        return {
            "band": lax.rem(band_me + step // n, bands),
            "grid": lax.rem(me + lax.rem(step, n), n),
        }

    def greet(step, carry):
        pl.semaphore_signal(barrier, inc=1, device_id=other(step), device_id_type=MESH)
        return carry

    lax.fori_loop(1, n * bands, greet, 0)
    keep = [
        pltpu.make_async_copy(source, target, sems_keep.at[place])
        for place, (source, target) in enumerate(
            ((orbital_hbm, raw_ref), (pivot_hbm, pivot_ref), (table_hbm, table_ref), (pattern_hbm, pattern_ref))
        )
    ]
    for copy in keep:
        copy.start()

    tile = picks.shape
    sublane = lax.broadcasted_iota(jnp.int32, tile, 0)
    lane = lax.broadcasted_iota(jnp.int32, tile, 1)
    keep[0].wait()
    keep[1].wait()
    slab = planes * length * length
    sampled = jnp.zeros((1, length), jnp.float32)
    for column in range(bands):
        cell = pivot_ref[column] - me * slab
        inside = jnp.where((cell >= 0) & (cell < slab), 1, 0)
        cell = jnp.clip(cell, 0, slab - 1)
        row = raw_ref[cell // (length * length), pl.ds(lax.rem(cell // length, length), 1), :]
        chosen = (lane[:1] == lax.rem(cell, length)) & (jnp.full((1, length), inside) > 0)
        value = jnp.sum(jnp.where(chosen, row, 0.0), axis=1, keepdims=True)
        sampled = sampled + jnp.where(lane[:1] == column, value, 0.0)
    picks[...] = jnp.where(sublane == band_me, jnp.broadcast_to(sampled, tile), 0.0)
    pl.semaphore_wait(barrier, n * bands - 1)

    def tell(step, carry):
        pltpu.make_async_remote_copy(
            src_ref=picks,
            dst_ref=told.at[step - 1],
            send_sem=sems_pick.at[0],
            recv_sem=sems_pick.at[1],
            device_id=other(step),
            device_id_type=MESH,
        ).start()
        return carry

    lax.fori_loop(1, n * bands, tell, 0)

    def part_copy(source, part, slot, target, passed):
        place = pl.ds(ahead_starts[part], ahead_sizes[part])
        return pltpu.make_async_remote_copy(
            src_ref=source.at[place],
            dst_ref=every_ref.at[slot, place],
            send_sem=sems_sent.at[0],
            recv_sem=sems_in.at[part, passed],
            device_id={"band": target},
            device_id_type=MESH,
        )

    def direct_copies(part):
        return [part_copy(raw_ref, part, slot, target, 0) for slot, target in enumerate(peers + [partner])]

    def passed_copies(part):
        return [
            part_copy(every_ref.at[step - 1], part, chips - 1 + step, partner, 1) for step in range(1, chips)
        ]

    for part in range(min(4, ahead_chunks)):
        for copy in direct_copies(part):
            copy.start()

    waves = [wrapped(lax.broadcasted_iota(jnp.int32, (length, length), axis), length) for axis in range(2)]
    base_ref[...] = waves[0] * waves[0] + waves[1] * waves[1]
    keep[3].wait()
    firsts = [[0.0] * bands for _ in range(2)]
    seconds = [0.0] * bands
    before = 0
    for row in range(bands):
        for column in range(bands):
            if row != column:
                on = jnp.where(pattern_ref[row, column] == 1, 1, 0)
                for place, band in enumerate((band_me, partner)):
                    chosen = jnp.where((on == 1) & (before == band), 1.0, 0.0)
                    firsts[place][row] = firsts[place][row] + chosen
                    if place == 0:
                        seconds[column] = seconds[column] + chosen
                before = before + on
    for place in range(2):
        for band in range(bands):
            share_ref[place, band] = firsts[place][band]

    await_bytes(told, sems_pick.at[1])
    total = picks[...] + jnp.sum(told[...], axis=0)
    columns_of = [
        jnp.broadcast_to(
            jnp.sum(jnp.where(lane == column, total, 0.0), axis=1, keepdims=True), tile
        )
        for column in range(bands)
    ]
    factor = [[None] * bands for _ in range(bands)]
    solved = []
    for row in range(bands):
        for column in range(row + 1):
            value = jnp.sum(columns_of[row] * columns_of[column], axis=0, keepdims=True)
            for step in range(column):
                value = value - factor[row][step] * factor[column][step]
            factor[row][column] = jnp.sqrt(value) if row == column else value / factor[column][column]
        value = columns_of[row]
        for step in range(row):
            value = value - factor[row][step] * solved[step]
        solved.append(value / factor[row][row])
    owns = [jnp.where(band_me == band, 1.0, 0.0) for band in range(bands)]
    for kind, weights in enumerate((owns, firsts[0], seconds)):
        value = weights[0] * solved[0]
        for band in range(1, bands):
            value = value + weights[band] * solved[band]
        mix_ref[kind] = value
    keep[2].wait()
    high, low = table_ref[0], table_ref[1]
    ends = ((0, high), (length, low))
    for start, value in ends:
        for other in (0, length):
            left_ref[pl.ds(start, length), pl.ds(other, length)] = value
            right_ref[pl.ds(other, length), pl.ds(start, length)] = value

    def out_copies(part, half):
        start, step_size = ahead_starts[part] * rows, ahead_sizes[part] * rows
        mine = pl.ds(pl.multiple_of(me * size + start, 8), step_size)
        copies = []
        for step in range(1, n):
            target = lax.rem(me + step, n)
            copies.append(
                pltpu.make_async_remote_copy(
                    src_ref=send_one.at[target, half, :, pl.ds(start, step_size), :],
                    dst_ref=recv_one.at[half, :, mine, :],
                    send_sem=sems_sent.at[1],
                    recv_sem=sems_one.at[part, half],
                    device_id={"grid": target},
                    device_id_type=MESH,
                )
            )
        return copies

    def own_copy(half):
        return pltpu.make_async_copy(
            send_one.at[me, half],
            recv_one.at[half, :, pl.ds(pl.multiple_of(me * size, size), size), :],
            sems_own.at[half],
        )

    def back_copies(part, half):
        start, step_size = back_starts[part] * rows, back_sizes[part] * rows
        copies = []
        for step in range(1, n):
            target = lax.rem(me + step, n)
            place = pl.ds(pl.multiple_of(target * size + start, 8), step_size)
            copies.append(
                pltpu.make_async_remote_copy(
                    src_ref=send_two.at[half, :, place, :],
                    dst_ref=recv_two.at[half, me, :, pl.ds(start, step_size), :],
                    send_sem=sems_sent.at[2],
                    recv_sem=sems_two.at[part, half],
                    device_id={"grid": target},
                    device_id_type=MESH,
                )
            )
        return copies

    def own_back(half):
        return pltpu.make_async_copy(
            send_two.at[half, :, pl.ds(pl.multiple_of(me * size, size), size), :],
            recv_two.at[half, me],
            sems_own.at[halves + half],
        )

    def ahead(plane, carry):
        values = [raw_ref[plane]] + [every_ref[slot, plane] for slot in range(bands - 1)]
        parts = []
        for kind in range(3):
            value = mix_ref[kind, pl.ds(band_me, 1), :] * values[0]
            for slot in range(bands - 1):
                value = value + mix_ref[kind, pl.ds(slots[slot], 1), :] * values[slot + 1]
            parts.append(value)
        own, first, second = parts
        own_ref[plane] = own
        second_ref[plane] = second
        both = jnp.concatenate([own * own, first * second], axis=0)
        spectrum = along_lanes(both, right_ref[...])
        result = along_rows(
            jnp.concatenate([spectrum[:length], spectrum[length:]], axis=1), left_ref[...]
        )
        for target in range(n):
            for half in range(halves):
                for part in range(2):
                    low = target * depth + half * rows
                    send_one[target, half, part, pl.ds(plane * rows, rows), :] = (
                        result[low : low + rows, part * length : (part + 1) * length]
                    )
        return carry

    def columns(half):
        def step(row, carry):
            place = pl.ds(row, length, stride=rows)
            both = jnp.concatenate(
                [recv_one[half, 0, place, :], recv_one[half, 1, place, :]], axis=1
            )
            wave = wrapped(me * depth + half * rows + row, length)
            squared = base_ref[...] + wave * wave
            scaling = float(length) ** 1.5
            weights = jnp.where(
                squared > 0, 0.25 / (scaling * jnp.maximum(squared, 1.0)), 0.0
            )
            spectrum = along_rows(both, left_ref[...])
            spectrum = spectrum * jnp.concatenate([weights, weights], axis=1)
            result = along_rows(spectrum, left_ref[...])
            send_two[half, 0, place, :] = result[:, :length]
            send_two[half, 1, place, :] = result[:, length:]
            return carry

        lax.fori_loop(0, rows, step, 0)
        own_back(half).start()

    def twin_copy(part):
        place = pl.ds(back_starts[part], back_sizes[part])
        return pltpu.make_async_remote_copy(
            src_ref=off_ref.at[place],
            dst_ref=twin_ref.at[place],
            send_sem=sems_sent.at[3],
            recv_sem=sems_twin.at[part],
            device_id={"band": partner},
            device_id_type=MESH,
        )

    def chip_copies(part):
        place = pl.ds(back_starts[part], back_sizes[part])
        return [
            pltpu.make_async_remote_copy(
                src_ref=going.at[step, place],
                dst_ref=coming.at[step, place],
                send_sem=sems_sent.at[4],
                recv_sem=sems_chip.at[part],
                device_id={"band": peer},
                device_id_type=MESH,
            )
            for step, peer in enumerate(peers)
        ]

    def shared(part):
        await_bytes(twin_ref.at[pl.ds(back_starts[part], back_sizes[part])], sems_twin.at[part])

        def one(plane, carry):
            mine, other = off_ref[plane], twin_ref[plane]
            for step, peer in enumerate(peers):
                going[step, plane] = share_ref[0, peer] * mine + share_ref[1, peer] * other
            term_ref[plane] = (
                term_ref[plane] + share_ref[0, band_me] * mine + share_ref[1, band_me] * other
            )
            return carry

        lax.fori_loop(back_starts[part], back_starts[part + 1], one, 0)
        for copy in chip_copies(part):
            copy.start()

    def home(plane, carry):
        place = pl.ds(plane * rows, rows)
        both = jnp.concatenate(
            [
                jnp.concatenate(
                    [recv_two[half, source, part, place, :] for source in range(n) for half in range(halves)],
                    axis=0,
                )
                for part in range(2)
            ],
            axis=1,
        )
        result = along_rows(both, left_ref[...])
        potential = along_lanes(
            jnp.concatenate([result[:, :length], result[:, length:]], axis=0), right_ref[...]
        )
        term_ref[plane] = potential[:length] * own_ref[plane]
        off_ref[plane] = potential[length:] * second_ref[plane]
        return carry

    def last(plane, carry):
        total = term_ref[plane]
        for step in range(chips - 1):
            total = total + coming[step, plane]
        term_ref[plane] = total
        return carry

    def copies_of(piece):
        kind, part, half = piece
        return back_copies(part, half) if kind else out_copies(part, half)

    forward, late = [], []
    for part in range(ahead_chunks):
        forward.append((0, part, 0))
        late.extend((0, part, half) for half in range(1, halves))
        if part % 2 == 1 and part < ahead_chunks - 1 and late:
            forward.append(late.pop(0))
    forward = forward + late
    backward = []
    for place in range(back_chunks + lag * (halves - 1)):
        for half in range(halves):
            if 0 <= place - lag * half < back_chunks:
                backward.append((1, place - lag * half, half))
    pieces = forward + backward
    arrived, filtered, finished = set(), set(), set()

    def arrive(piece):
        if piece not in arrived:
            arrived.add(piece)
            kind, part, half = piece
            if kind:
                taken = pl.ds(0, back_sizes[part] * rows)
                await_bytes(recv_two.at[half, pl.ds(0, n - 1), :, taken, :], sems_two.at[part, half])
            else:
                taken = pl.ds(0, (n - 1) * ahead_sizes[part] * rows)
                await_bytes(recv_one.at[half, :, taken, :], sems_one.at[part, half])

    def filter_half(half):
        if half not in filtered:
            filtered.add(half)
            for part in range(ahead_chunks):
                arrive((0, part, half))
            own_copy(half).wait()
            columns(half)

    def finish(part):
        finished.add(part)
        if len(finished) == 1:
            for half in range(halves):
                own_back(half).wait()
        for half in range(halves):
            arrive((1, part, half))
        lax.fori_loop(back_starts[part], back_starts[part + 1], home, 0)
        twin_copy(part).start()
        shared(part)

    ready = 0
    for index, piece in enumerate(pieces):
        kind, part, half = piece
        if index >= window:
            arrive(pieces[index - window])
        if kind == 0 and part == ready:
            ready += 1
            place = pl.ds(ahead_starts[part], ahead_sizes[part])
            await_bytes(every_ref.at[pl.ds(0, chips), place], sems_in.at[part, 0])
            for copy in passed_copies(part):
                copy.start()
            if part + 4 < ahead_chunks:
                for copy in direct_copies(part + 4):
                    copy.start()
            await_bytes(every_ref.at[pl.ds(chips, chips - 1), place], sems_in.at[part, 1])
            lax.fori_loop(ahead_starts[part], ahead_starts[part + 1], ahead, 0)
            if ready == ahead_chunks:
                for each in range(halves):
                    own_copy(each).start()
        if kind == 1:
            filter_half(half)
        for copy in copies_of(piece):
            copy.start()
        for each in range(halves):
            if ready == ahead_chunks and all((0, p, each) in arrived for p in range(ahead_chunks)):
                filter_half(each)
        for each in range(back_chunks):
            if each not in finished and all((1, each, h) in arrived for h in range(halves)):
                finish(each)
    for piece in pieces:
        arrive(piece)
        for each in range(back_chunks):
            if each not in finished and all((1, each, h) in arrived for h in range(halves)):
                finish(each)
    for part in range(back_chunks):
        place = pl.ds(back_starts[part], back_sizes[part])
        await_bytes(coming.at[:, place], sems_chip.at[part])
        lax.fori_loop(back_starts[part], back_starts[part + 1], last, 0)
    await_bytes(told, sems_pick.at[0])
    await_bytes(every_ref, sems_sent.at[0])
    await_bytes(send_one.at[pl.ds(0, n - 1)], sems_sent.at[1])
    await_bytes(send_two.at[:, :, pl.ds(0, (n - 1) * size), :], sems_sent.at[2])
    await_bytes(off_ref, sems_sent.at[3])
    await_bytes(going, sems_sent.at[4])


def local(orbitals, pivots, pattern):
    orbital = orbitals[0]
    n, bands = lax.axis_size("grid"), lax.axis_size("band")
    planes, length = orbital.shape[0], orbital.shape[2]
    chips = bands // 2
    depth = length // n
    halves = 2 if depth % 16 == 0 else 1
    rows = depth // halves
    unit = planes // 16
    small = (2,) * (planes // 2)
    ahead_sizes = tuple(unit * size for size in (1, 1, 2, 2, 2, 2, 2, 2, 2)) if unit else small
    back_sizes = tuple(unit * size for size in (2, 2, 2, 2, 2, 2, 2, 1, 1)) if unit else small
    ahead_chunks, back_chunks = len(ahead_sizes), len(back_sizes)
    table = hartley_table(length)
    hbm = pl.BlockSpec(memory_space=pl.ANY)
    vmem = pl.BlockSpec(memory_space=pltpu.VMEM)
    slab = pltpu.VMEM(orbital.shape, jnp.float32)
    block = planes * rows
    tile = (-(-bands // 8) * 8, length)
    dma = pltpu.SemaphoreType.DMA
    localized, exchange_term = pl.pallas_call(
        functools.partial(transform_kernel, n, halves, ahead_sizes, back_sizes, chips, 4, 3),
        out_shape=(slab, slab),
        in_specs=[hbm] * 4,
        out_specs=(vmem, vmem),
        scratch_shapes=[
            pltpu.VMEM((n, halves, 2, block, length), jnp.float32),
            pltpu.VMEM((halves, 2, n * block, length), jnp.float32),
            pltpu.VMEM((halves, 2, n * block, length), jnp.float32),
            pltpu.VMEM((halves, n, 2, block, length), jnp.float32),
            pltpu.VMEM(slab.shape, jnp.float32),
            pltpu.VMEM(slab.shape, jnp.float32),
            pltpu.VMEM(slab.shape, jnp.float32),
            pltpu.VMEM((chips - 1,) + slab.shape, jnp.float32),
            pltpu.VMEM((chips - 1,) + slab.shape, jnp.float32),
            pltpu.VMEM((bands - 1,) + slab.shape, jnp.float32),
            pltpu.VMEM(slab.shape, jnp.float32),
            pltpu.VMEM((2 * length, 2 * length), table.dtype),
            pltpu.VMEM((2 * length, 2 * length), table.dtype),
            pltpu.VMEM((length, length), jnp.float32),
            pltpu.VMEM(tile, jnp.float32),
            pltpu.VMEM((n * bands - 1,) + tile, jnp.float32),
            pltpu.VMEM((3,) + tile, jnp.float32),
            pltpu.SMEM((2, bands), jnp.float32),
            pltpu.VMEM(table.shape, table.dtype),
            pltpu.SMEM(pivots.shape, jnp.int32),
            pltpu.SMEM(pattern.shape, jnp.int32),
            dma((ahead_chunks, halves)),
            dma((back_chunks, halves)),
            dma((2 * halves,)),
            dma((back_chunks,)),
            dma((back_chunks,)),
            dma((ahead_chunks, 2)),
            dma((4,)),
            dma((5,)),
            dma((2,)),
        ],
        compiler_params=pltpu.CompilerParams(
            collective_id=0, has_side_effects=True, vmem_limit_bytes=56 * 1024 * 1024
        ),
    )(pivots, pattern, orbital, table)
    return (localized[None], exchange_term[None])


def solution(mesh):
    return jax.shard_map(
        local,
        mesh=mesh,
        in_specs=(P("band", "grid", None, None), P(), P()),
        out_specs=(P("band", "grid", None, None), P("band", "grid", None, None)),
        check_vma=False,
    )
```

```python
import functools

import jax
import jax.numpy as jnp
import numpy as np
from jax import lax
from jax.experimental import pallas as pl
from jax.experimental.pallas import tpu as pltpu
from jax.sharding import PartitionSpec as P

MESH = pl.DeviceIdType.MESH


def hartley_table(length):
    across = np.arange(length)
    angles = (across[:, None] * across[None, :] % length) * (2.0 * np.pi / length)
    table = np.cos(angles) + np.sin(angles)
    high = table.astype(jnp.bfloat16)
    low = (table - high.astype(np.float64)).astype(jnp.bfloat16)
    return jnp.asarray(np.stack([high, low]))


def await_bytes(ref, sem):
    pltpu.make_async_copy(ref, ref, sem).wait()


def in_two(values, axis):
    high = values.astype(jnp.bfloat16)
    low = (values - high.astype(jnp.float32)).astype(jnp.bfloat16)
    return jnp.concatenate([high, low], axis=axis)


def along_lanes(values, table):
    length = values.shape[1]
    both = jnp.dot(in_two(values, 1), table, preferred_element_type=jnp.float32)
    return both[:, :length] + both[:, length:]


def along_rows(values, table):
    length = values.shape[0]
    both = jnp.dot(table, in_two(values, 0), preferred_element_type=jnp.float32)
    return both[:length] + both[length:]


def wrapped(indices, length):
    return jnp.where(indices < length // 2, indices, indices - length).astype(jnp.float32)


def transform_kernel(
    n, halves, ahead_sizes, back_sizes, chips, window, lag,
    pivot_hbm, pattern_hbm, orbital_hbm, table_hbm,
    own_ref, term_ref,
    send_one, recv_one, send_two, recv_two, second_ref, off_ref, twin_ref, going, coming,
    every_ref, raw_ref, left_ref, right_ref, base_ref, picks, told, mix_ref, share_ref,
    table_ref, pivot_ref, pattern_ref,
    sems_one, sems_two, sems_own, sems_twin, sems_chip, sems_in, sems_keep, sems_sent, sems_pick,
):
    bands = every_ref.shape[0] + 1
    planes, length = own_ref.shape[0], own_ref.shape[2]
    me, band_me = lax.axis_index("grid"), lax.axis_index("band")
    chip, core = band_me // 2, lax.rem(band_me, 2)
    partner = chip * 2 + 1 - core
    peers = [lax.rem(chip + step, chips) * 2 + core for step in range(1, chips)]
    sources = [lax.rem(chip + chips - step, chips) * 2 for step in range(1, chips)]
    slots = [low + core for low in sources] + [partner] + [low + 1 - core for low in sources]
    depth = length // n
    rows = depth // halves
    size = planes * rows
    ahead_chunks, back_chunks = len(ahead_sizes), len(back_sizes)
    ahead_starts = [sum(ahead_sizes[:part]) for part in range(ahead_chunks + 1)]
    back_starts = [sum(back_sizes[:part]) for part in range(back_chunks + 1)]
    barrier = pltpu.get_barrier_semaphore()

    def other(step):
        return {
            "band": lax.rem(band_me + step // n, bands),
            "grid": lax.rem(me + lax.rem(step, n), n),
        }

    def greet(step, carry):
        pl.semaphore_signal(barrier, inc=1, device_id=other(step), device_id_type=MESH)
        return carry

    lax.fori_loop(1, n * bands, greet, 0)
    keep = [
        pltpu.make_async_copy(source, target, sems_keep.at[place])
        for place, (source, target) in enumerate(
            ((orbital_hbm, raw_ref), (pivot_hbm, pivot_ref), (table_hbm, table_ref), (pattern_hbm, pattern_ref))
        )
    ]
    for copy in keep:
        copy.start()

    tile = picks.shape
    sublane = lax.broadcasted_iota(jnp.int32, tile, 0)
    lane = lax.broadcasted_iota(jnp.int32, tile, 1)
    keep[0].wait()
    keep[1].wait()
    slab = planes * length * length
    sampled = jnp.zeros((1, length), jnp.float32)
    for column in range(bands):
        cell = pivot_ref[column] - me * slab
        inside = jnp.where((cell >= 0) & (cell < slab), 1, 0)
        cell = jnp.clip(cell, 0, slab - 1)
        row = raw_ref[cell // (length * length), pl.ds(lax.rem(cell // length, length), 1), :]
        chosen = (lane[:1] == lax.rem(cell, length)) & (jnp.full((1, length), inside) > 0)
        value = jnp.sum(jnp.where(chosen, row, 0.0), axis=1, keepdims=True)
        sampled = sampled + jnp.where(lane[:1] == column, value, 0.0)
    picks[...] = jnp.where(sublane == band_me, jnp.broadcast_to(sampled, tile), 0.0)
    pl.semaphore_wait(barrier, n * bands - 1)

    def tell(step, carry):
        pltpu.make_async_remote_copy(
            src_ref=picks,
            dst_ref=told.at[step - 1],
            send_sem=sems_pick.at[0],
            recv_sem=sems_pick.at[1],
            device_id=other(step),
            device_id_type=MESH,
        ).start()
        return carry

    lax.fori_loop(1, n * bands, tell, 0)

    def part_copy(source, part, slot, target, passed):
        place = pl.ds(ahead_starts[part], ahead_sizes[part])
        return pltpu.make_async_remote_copy(
            src_ref=source.at[place],
            dst_ref=every_ref.at[slot, place],
            send_sem=sems_sent.at[0],
            recv_sem=sems_in.at[part, passed],
            device_id={"band": target},
            device_id_type=MESH,
        )

    def direct_copies(part):
        return [part_copy(raw_ref, part, slot, target, 0) for slot, target in enumerate(peers + [partner])]

    def passed_copies(part):
        return [
            part_copy(every_ref.at[step - 1], part, chips - 1 + step, partner, 1) for step in range(1, chips)
        ]

    for part in range(min(4, ahead_chunks)):
        for copy in direct_copies(part):
            copy.start()

    waves = [wrapped(lax.broadcasted_iota(jnp.int32, (length, length), axis), length) for axis in range(2)]
    base_ref[...] = waves[0] * waves[0] + waves[1] * waves[1]
    keep[3].wait()
    firsts = [[0.0] * bands for _ in range(2)]
    seconds = [0.0] * bands
    before = 0
    for row in range(bands):
        for column in range(bands):
            if row != column:
                on = jnp.where(pattern_ref[row, column] == 1, 1, 0)
                for place, band in enumerate((band_me, partner)):
                    chosen = jnp.where((on == 1) & (before == band), 1.0, 0.0)
                    firsts[place][row] = firsts[place][row] + chosen
                    if place == 0:
                        seconds[column] = seconds[column] + chosen
                before = before + on
    for place in range(2):
        for band in range(bands):
            share_ref[place, band] = firsts[place][band]

    await_bytes(told, sems_pick.at[1])
    total = picks[...] + jnp.sum(told[...], axis=0)
    columns_of = [
        jnp.broadcast_to(
            jnp.sum(jnp.where(lane == column, total, 0.0), axis=1, keepdims=True), tile
        )
        for column in range(bands)
    ]
    factor = [[None] * bands for _ in range(bands)]
    solved = []
    for row in range(bands):
        for column in range(row + 1):
            value = jnp.sum(columns_of[row] * columns_of[column], axis=0, keepdims=True)
            for step in range(column):
                value = value - factor[row][step] * factor[column][step]
            factor[row][column] = jnp.sqrt(value) if row == column else value / factor[column][column]
        value = columns_of[row]
        for step in range(row):
            value = value - factor[row][step] * solved[step]
        solved.append(value / factor[row][row])
    owns = [jnp.where(band_me == band, 1.0, 0.0) for band in range(bands)]
    for kind, weights in enumerate((owns, firsts[0], seconds)):
        value = weights[0] * solved[0]
        for band in range(1, bands):
            value = value + weights[band] * solved[band]
        mix_ref[kind] = value
    keep[2].wait()
    high, low = table_ref[0], table_ref[1]
    ends = ((0, high), (length, low))
    for start, value in ends:
        for other in (0, length):
            left_ref[pl.ds(start, length), pl.ds(other, length)] = value
            right_ref[pl.ds(other, length), pl.ds(start, length)] = value

    def out_copies(part, half):
        start, step_size = ahead_starts[part] * rows, ahead_sizes[part] * rows
        mine = pl.ds(pl.multiple_of(me * size + start, 8), step_size)
        copies = []
        for step in range(1, n):
            target = lax.rem(me + step, n)
            copies.append(
                pltpu.make_async_remote_copy(
                    src_ref=send_one.at[target, half, :, pl.ds(start, step_size), :],
                    dst_ref=recv_one.at[half, :, mine, :],
                    send_sem=sems_sent.at[1],
                    recv_sem=sems_one.at[part, half],
                    device_id={"grid": target},
                    device_id_type=MESH,
                )
            )
        return copies

    def own_copy(half):
        return pltpu.make_async_copy(
            send_one.at[me, half],
            recv_one.at[half, :, pl.ds(pl.multiple_of(me * size, size), size), :],
            sems_own.at[half],
        )

    def back_copies(part, half):
        start, step_size = back_starts[part] * rows, back_sizes[part] * rows
        copies = []
        for step in range(1, n):
            target = lax.rem(me + step, n)
            place = pl.ds(pl.multiple_of(target * size + start, 8), step_size)
            copies.append(
                pltpu.make_async_remote_copy(
                    src_ref=send_two.at[half, :, place, :],
                    dst_ref=recv_two.at[half, me, :, pl.ds(start, step_size), :],
                    send_sem=sems_sent.at[2],
                    recv_sem=sems_two.at[part, half],
                    device_id={"grid": target},
                    device_id_type=MESH,
                )
            )
        return copies

    def own_back(half):
        return pltpu.make_async_copy(
            send_two.at[half, :, pl.ds(pl.multiple_of(me * size, size), size), :],
            recv_two.at[half, me],
            sems_own.at[halves + half],
        )

    def ahead(plane, carry):
        values = [raw_ref[plane]] + [every_ref[slot, plane] for slot in range(bands - 1)]
        parts = []
        for kind in range(3):
            value = mix_ref[kind, pl.ds(band_me, 1), :] * values[0]
            for slot in range(bands - 1):
                value = value + mix_ref[kind, pl.ds(slots[slot], 1), :] * values[slot + 1]
            parts.append(value)
        own, first, second = parts
        own_ref[plane] = own
        second_ref[plane] = second
        both = jnp.concatenate([own * own, first * second], axis=0)
        spectrum = along_lanes(both, right_ref[...])
        result = along_rows(
            jnp.concatenate([spectrum[:length], spectrum[length:]], axis=1), left_ref[...]
        )
        for target in range(n):
            for half in range(halves):
                for part in range(2):
                    low = target * depth + half * rows
                    send_one[target, half, part, pl.ds(plane * rows, rows), :] = (
                        result[low : low + rows, part * length : (part + 1) * length]
                    )
        return carry

    def columns(half):
        def step(row, carry):
            place = pl.ds(row, length, stride=rows)
            both = jnp.concatenate(
                [recv_one[half, 0, place, :], recv_one[half, 1, place, :]], axis=1
            )
            wave = wrapped(me * depth + half * rows + row, length)
            squared = base_ref[...] + wave * wave
            scaling = float(length) ** 1.5
            weights = jnp.where(
                squared > 0, 0.25 / (scaling * jnp.maximum(squared, 1.0)), 0.0
            )
            spectrum = along_rows(both, left_ref[...])
            spectrum = spectrum * jnp.concatenate([weights, weights], axis=1)
            result = along_rows(spectrum, left_ref[...])
            send_two[half, 0, place, :] = result[:, :length]
            send_two[half, 1, place, :] = result[:, length:]
            return carry

        lax.fori_loop(0, rows, step, 0)
        own_back(half).start()

    def twin_copy(part):
        place = pl.ds(back_starts[part], back_sizes[part])
        return pltpu.make_async_remote_copy(
            src_ref=off_ref.at[place],
            dst_ref=twin_ref.at[place],
            send_sem=sems_sent.at[3],
            recv_sem=sems_twin.at[part],
            device_id={"band": partner},
            device_id_type=MESH,
        )

    def chip_copies(part):
        place = pl.ds(back_starts[part], back_sizes[part])
        return [
            pltpu.make_async_remote_copy(
                src_ref=going.at[step, place],
                dst_ref=coming.at[step, place],
                send_sem=sems_sent.at[4],
                recv_sem=sems_chip.at[part],
                device_id={"band": peer},
                device_id_type=MESH,
            )
            for step, peer in enumerate(peers)
        ]

    def shared(part):
        await_bytes(twin_ref.at[pl.ds(back_starts[part], back_sizes[part])], sems_twin.at[part])

        def one(plane, carry):
            mine, other = off_ref[plane], twin_ref[plane]
            for step, peer in enumerate(peers):
                going[step, plane] = share_ref[0, peer] * mine + share_ref[1, peer] * other
            term_ref[plane] = (
                term_ref[plane] + share_ref[0, band_me] * mine + share_ref[1, band_me] * other
            )
            return carry

        lax.fori_loop(back_starts[part], back_starts[part + 1], one, 0, unroll=True)
        for copy in chip_copies(part):
            copy.start()

    def home(plane, carry):
        place = pl.ds(plane * rows, rows)
        both = jnp.concatenate(
            [
                jnp.concatenate(
                    [recv_two[half, source, part, place, :] for source in range(n) for half in range(halves)],
                    axis=0,
                )
                for part in range(2)
            ],
            axis=1,
        )
        result = along_rows(both, left_ref[...])
        potential = along_lanes(
            jnp.concatenate([result[:, :length], result[:, length:]], axis=0), right_ref[...]
        )
        term_ref[plane] = potential[:length] * own_ref[plane]
        off_ref[plane] = potential[length:] * second_ref[plane]
        return carry

    def last(plane, carry):
        total = term_ref[plane]
        for step in range(chips - 1):
            total = total + coming[step, plane]
        term_ref[plane] = total
        return carry

    def copies_of(piece):
        kind, part, half = piece
        return back_copies(part, half) if kind else out_copies(part, half)

    forward, late = [], []
    for part in range(ahead_chunks):
        forward.append((0, part, 0))
        late.extend((0, part, half) for half in range(1, halves))
        if part % 2 == 1 and part < ahead_chunks - 1 and late:
            forward.append(late.pop(0))
    forward = forward + late
    backward = []
    for place in range(back_chunks + lag * (halves - 1)):
        for half in range(halves):
            if 0 <= place - lag * half < back_chunks:
                backward.append((1, place - lag * half, half))
    pieces = forward + backward
    arrived, filtered, finished = set(), set(), set()

    def arrive(piece):
        if piece not in arrived:
            arrived.add(piece)
            kind, part, half = piece
            if kind:
                taken = pl.ds(0, back_sizes[part] * rows)
                await_bytes(recv_two.at[half, pl.ds(0, n - 1), :, taken, :], sems_two.at[part, half])
            else:
                taken = pl.ds(0, (n - 1) * ahead_sizes[part] * rows)
                await_bytes(recv_one.at[half, :, taken, :], sems_one.at[part, half])

    def filter_half(half):
        if half not in filtered:
            filtered.add(half)
            for part in range(ahead_chunks):
                arrive((0, part, half))
            own_copy(half).wait()
            columns(half)

    def finish(part):
        finished.add(part)
        if len(finished) == 1:
            for half in range(halves):
                own_back(half).wait()
        for half in range(halves):
            arrive((1, part, half))
        lax.fori_loop(back_starts[part], back_starts[part + 1], home, 0, unroll=True)
        twin_copy(part).start()
        shared(part)

    ready = 0
    for index, piece in enumerate(pieces):
        kind, part, half = piece
        if index >= window:
            arrive(pieces[index - window])
        if kind == 0 and part == ready:
            ready += 1
            place = pl.ds(ahead_starts[part], ahead_sizes[part])
            await_bytes(every_ref.at[pl.ds(0, chips), place], sems_in.at[part, 0])
            for copy in passed_copies(part):
                copy.start()
            if part + 4 < ahead_chunks:
                for copy in direct_copies(part + 4):
                    copy.start()
            await_bytes(every_ref.at[pl.ds(chips, chips - 1), place], sems_in.at[part, 1])
            lax.fori_loop(ahead_starts[part], ahead_starts[part + 1], ahead, 0)
            if ready == ahead_chunks:
                for each in range(halves):
                    own_copy(each).start()
        if kind == 1:
            filter_half(half)
        for copy in copies_of(piece):
            copy.start()
        for each in range(halves):
            if ready == ahead_chunks and all((0, p, each) in arrived for p in range(ahead_chunks)):
                filter_half(each)
        for each in range(back_chunks):
            if each not in finished and all((1, each, h) in arrived for h in range(halves)):
                finish(each)
    for piece in pieces:
        arrive(piece)
        for each in range(back_chunks):
            if each not in finished and all((1, each, h) in arrived for h in range(halves)):
                finish(each)
    for part in range(back_chunks):
        place = pl.ds(back_starts[part], back_sizes[part])
        await_bytes(coming.at[:, place], sems_chip.at[part])
        lax.fori_loop(back_starts[part], back_starts[part + 1], last, 0, unroll=True)
    await_bytes(told, sems_pick.at[0])
    await_bytes(every_ref, sems_sent.at[0])
    await_bytes(send_one.at[pl.ds(0, n - 1)], sems_sent.at[1])
    await_bytes(send_two.at[:, :, pl.ds(0, (n - 1) * size), :], sems_sent.at[2])
    await_bytes(off_ref, sems_sent.at[3])
    await_bytes(going, sems_sent.at[4])


def local(orbitals, pivots, pattern):
    orbital = orbitals[0]
    n, bands = lax.axis_size("grid"), lax.axis_size("band")
    planes, length = orbital.shape[0], orbital.shape[2]
    chips = bands // 2
    depth = length // n
    halves = 2 if depth % 16 == 0 else 1
    rows = depth // halves
    unit = planes // 16
    small = (2,) * (planes // 2)
    ahead_sizes = tuple(unit * size for size in (1, 1, 2, 2, 2, 2, 2, 2, 2)) if unit else small
    back_sizes = tuple(unit * size for size in (2, 2, 2, 2, 2, 2, 2, 1, 1)) if unit else small
    ahead_chunks, back_chunks = len(ahead_sizes), len(back_sizes)
    table = hartley_table(length)
    hbm = pl.BlockSpec(memory_space=pl.ANY)
    vmem = pl.BlockSpec(memory_space=pltpu.VMEM)
    slab = pltpu.VMEM(orbital.shape, jnp.float32)
    block = planes * rows
    tile = (-(-bands // 8) * 8, length)
    dma = pltpu.SemaphoreType.DMA
    localized, exchange_term = pl.pallas_call(
        functools.partial(transform_kernel, n, halves, ahead_sizes, back_sizes, chips, 4, 3),
        out_shape=(slab, slab),
        in_specs=[hbm] * 4,
        out_specs=(vmem, vmem),
        scratch_shapes=[
            pltpu.VMEM((n, halves, 2, block, length), jnp.float32),
            pltpu.VMEM((halves, 2, n * block, length), jnp.float32),
            pltpu.VMEM((halves, 2, n * block, length), jnp.float32),
            pltpu.VMEM((halves, n, 2, block, length), jnp.float32),
            pltpu.VMEM(slab.shape, jnp.float32),
            pltpu.VMEM(slab.shape, jnp.float32),
            pltpu.VMEM(slab.shape, jnp.float32),
            pltpu.VMEM((chips - 1,) + slab.shape, jnp.float32),
            pltpu.VMEM((chips - 1,) + slab.shape, jnp.float32),
            pltpu.VMEM((bands - 1,) + slab.shape, jnp.float32),
            pltpu.VMEM(slab.shape, jnp.float32),
            pltpu.VMEM((2 * length, 2 * length), table.dtype),
            pltpu.VMEM((2 * length, 2 * length), table.dtype),
            pltpu.VMEM((length, length), jnp.float32),
            pltpu.VMEM(tile, jnp.float32),
            pltpu.VMEM((n * bands - 1,) + tile, jnp.float32),
            pltpu.VMEM((3,) + tile, jnp.float32),
            pltpu.SMEM((2, bands), jnp.float32),
            pltpu.VMEM(table.shape, table.dtype),
            pltpu.SMEM(pivots.shape, jnp.int32),
            pltpu.SMEM(pattern.shape, jnp.int32),
            dma((ahead_chunks, halves)),
            dma((back_chunks, halves)),
            dma((2 * halves,)),
            dma((back_chunks,)),
            dma((back_chunks,)),
            dma((ahead_chunks, 2)),
            dma((4,)),
            dma((5,)),
            dma((2,)),
        ],
        compiler_params=pltpu.CompilerParams(
            collective_id=0, has_side_effects=True, vmem_limit_bytes=56 * 1024 * 1024
        ),
    )(pivots, pattern, orbital, table)
    return (localized[None], exchange_term[None])


def solution(mesh):
    return jax.shard_map(
        local,
        mesh=mesh,
        in_specs=(P("band", "grid", None, None), P(), P()),
        out_specs=(P("band", "grid", None, None), P("band", "grid", None, None)),
        check_vma=False,
    )
```
